32 devices in a mesh: region: 2 (over y), tile: 4 (over z), shot: 2 (over x), pair: 2 (over core).
Axes of the slice: x: 2, y: 2, z: 4, core: 2. Of those that a mesh axis runs over, the one named last changes fastest.
Arguments:
- velocity: float32 [64, 128, 128], P(('region', 'tile'), ('shot', 'pair')), parts along dimension 0, may hold values from 1.5 to 4.5
- anchors: int32 [4], P(('region', 'shot')), parts along dimension 0, may hold values from 0 to 64, as said below
- source_prev: float32 [8, 32, 64, 128], P(('region', 'shot', 'pair'), 'tile'), parts along dimension 0, may hold values from -6 to 6
- source_now: float32 [8, 32, 64, 128], P(('region', 'shot', 'pair'), 'tile'), parts along dimension 0, may hold values from -6 to 6
- recv_prev: float32 [8, 32, 64, 128], P(('region', 'shot', 'pair'), 'tile'), parts along dimension 0, may hold values from -6 to 6
- recv_now: float32 [8, 32, 64, 128], P(('region', 'shot', 'pair'), 'tile'), parts along dimension 0, may hold values from -6 to 6
- source_x: int32 [8], P(('region', 'shot', 'pair')), parts along dimension 0, may hold values from 0 to 31
- source_yz: int32 [8], P(('region', 'shot', 'pair')), parts along dimension 0, may hold values from 0 to 8191
- wavelet: float32 [8, 6], P(('region', 'shot', 'pair')), parts along dimension 0, may hold values from -6 to 6
- recv_x: int32 [8, 128], P(('region', 'shot', 'pair')), parts along dimension 0, may hold values from 0 to 31
- recv_yz: int32 [8, 128], P(('region', 'shot', 'pair')), parts along dimension 0, may hold values from 0 to 8191
- record: float32 [8, 6, 128], P(('region', 'shot', 'pair')), parts along dimension 0, may hold values from -6 to 6
Outputs:
- image: float32 [64, 128, 128], P(('region', 'tile'), ('shot', 'pair')), parts along dimension 0
- source_field: float32 [8, 32, 64, 128], P(('region', 'shot', 'pair'), 'tile'), parts along dimension 0
- receiver_field: float32 [8, 32, 64, 128], P(('region', 'shot', 'pair'), 'tile'), parts along dimension 0
The draws below stay inside these ranges and needn't reach their ends.
There are 2 independent parts, one for each index of `region`. The reference program is written for one: setup_inputs(seed, part) draws one part's arguments, and reference() takes and returns one part's arrays. A program takes and returns all parts, laid end to end along the dimension named above; each array names one. Nothing has to cross between parts.
Inputs may be any that keep to these rules, and one draw needn't show every extreme that they name: Aperture a covers survey rows anchors[a] to anchors[a] + 63 along the second dimension; in every draw some aperture starts at 64.
All inputs are finite; a program needn't handle non-finite values.
Results may differ from the reference program's by a relative error of at most 0.00002.
Values sent between devices are 32-bit elements; how exact they have to be, the bound alone decides.
A program may use at most 64 MiB of HBM per device.

```python
import jax
import jax.numpy as jnp
from jax import lax

Z = 128
STEPS = 6
NREC = 128
SHOTS = 4
APERTURES = 2
AX = 32
NYS = 128
AY = 64
N_PAIR = 2


def draw_anchors(key, part):
    highest = NYS - AY
    values = jax.random.randint(jax.random.fold_in(key, 11), (APERTURES,), 0, highest + 1, dtype=jnp.int32)
    chosen = jax.random.randint(jax.random.fold_in(key, 12), (), 0, APERTURES, dtype=jnp.int32)
    places = jnp.arange(APERTURES, dtype=jnp.int32)
    return jnp.where(places == chosen, highest, values).astype(jnp.int32)


def touch_ends(values, rng, smallest, high):
    extent = values.shape
    index_at = [jax.random.randint(jax.random.fold_in(rng, axis), (), 0, extent[axis]) for axis in range(len(extent))]
    values = values.at[tuple(index_at)].set(smallest)
    longest = extent.index(max(extent))
    index_at[longest] = (index_at[longest] + 1) % extent[longest]
    return values.at[tuple(index_at)].set(high)


def block_levels(stream_key, shape, split, low, top_value):
    level, own = 1.0, jax.random.fold_in(stream_key, 6)
    for axis_at, shards_of in split:
        steps = jnp.exp(jax.random.uniform(jax.random.fold_in(own, axis_at), (shards_of,), jnp.float32, low / len(split), top_value / len(split)))
        level = level * jnp.repeat(steps, shape[axis_at] // shards_of).reshape([-1 if axis == axis_at else 1 for axis in range(len(shape))])
    return level


def normal_values(key, extent, scale, bound, pieces=(), kind=jnp.bfloat16):
    loudness = block_levels(key, extent, pieces, -0.22, 0.18) if pieces else 1.0
    result = jax.random.normal(key, extent, jnp.float32) * scale * loudness
    return jnp.minimum(jnp.maximum(result, -bound), bound).astype(kind)


def setup_inputs(seed: int = 0, part: int = 0) -> dict:
    key_list = jax.random.split(jax.random.key(seed), 13)
    part_splits = jax.random.split(jax.random.fold_in(key_list[12], part), 13)
    return {
        "velocity": jnp.clip(1.5 + 3.0 * jax.random.uniform(part_splits[0], (AX, NYS, Z), jnp.float32) ** block_levels(part_splits[0], (AX, NYS, Z), ((0, 4), (1, 4)), -0.2, 0.2), 1.5, 4.5),
        "anchors": draw_anchors(jax.random.fold_in(jax.random.fold_in(key_list[12], part), 71), part),
        "source_prev": normal_values(part_splits[2], (SHOTS, AX, AY, Z), 1.0, 6.0, ((0, 4), (1, 4)), jnp.float32),
        "source_now": normal_values(part_splits[3], (SHOTS, AX, AY, Z), 1.0, 6.0, ((0, 4), (1, 4)), jnp.float32),
        "recv_prev": normal_values(part_splits[4], (SHOTS, AX, AY, Z), 1.0, 6.0, ((0, 4), (1, 4)), jnp.float32),
        "recv_now": normal_values(part_splits[5], (SHOTS, AX, AY, Z), 1.0, 6.0, ((0, 4), (1, 4)), jnp.float32),
        "source_x": touch_ends(jax.random.randint(part_splits[6], (SHOTS,), 0, AX), jax.random.fold_in(part_splits[6], 1), 0, AX - 1).astype(jnp.int32),
        "source_yz": touch_ends(jax.random.randint(part_splits[7], (SHOTS,), 0, AY * Z), jax.random.fold_in(part_splits[7], 1), 0, (AY * Z) - 1).astype(jnp.int32),
        "wavelet": normal_values(part_splits[8], (SHOTS, STEPS), 1.0, 6.0, ((0, 4),), jnp.float32),
        "recv_x": touch_ends(jax.random.randint(part_splits[9], (SHOTS, NREC), 0, AX), jax.random.fold_in(part_splits[9], 1), 0, AX - 1).astype(jnp.int32),
        "recv_yz": touch_ends(jax.random.randint(part_splits[10], (SHOTS, NREC), 0, AY * Z), jax.random.fold_in(part_splits[10], 1), 0, (AY * Z) - 1).astype(jnp.int32),
        "record": normal_values(part_splits[11], (SHOTS, STEPS, NREC), 1.0, 6.0, ((0, 4),), jnp.float32),
    }


stencil_weights = (-205.0 / 72.0, 8.0 / 5.0, -1.0 / 5.0, 8.0 / 315.0, -1.0 / 560.0)
courant_scale = 0.1


def laplace(extended):
    length = extended.shape[1]
    across = extended.shape[2]
    downward = extended.shape[3]
    interior = length - 8
    padded = jnp.pad(extended, ((0, 0), (0, 0), (4, 4), (4, 4)))

    def sample(along_x, along_y, along_z):
        return padded[:, 4 + along_x:4 + along_x + interior, 4 + along_y:4 + along_y + across, 4 + along_z:4 + along_z + downward]

    total = 3.0 * stencil_weights[0] * sample(0, 0, 0)
    for reach in range(1, 5):
        neighbour_sum = sample(reach, 0, 0) + sample(-reach, 0, 0) + sample(0, reach, 0) + sample(0, -reach, 0) + sample(0, 0, reach) + sample(0, 0, -reach)
        total = total + stencil_weights[reach] * neighbour_sum
    return total


def advance(older, current, courant):
    extended = jnp.pad(current, ((0, 0), (4, 4), (0, 0), (0, 0)))
    return 2.0 * current - older + courant * laplace(extended)


def deposit(fields, columns, planes, amounts):
    flat = fields.reshape(SHOTS, AX * AY * Z)
    shot_rows = jnp.zeros_like(columns) + jnp.arange(SHOTS, dtype=jnp.int32)[:, None]
    target = columns * (AY * Z) + planes
    return flat.at[shot_rows, target].add(amounts).reshape(fields.shape)


def reference(velocity, anchors, source_prev, source_now, recv_prev, recv_now, source_x, source_yz, wavelet, recv_x, recv_yz, record):
    starts = anchors.astype(jnp.int32)
    windows = [lax.dynamic_slice_in_dim(velocity, starts[member // N_PAIR], AY, 1) for member in range(SHOTS)]
    scaled = jnp.stack(windows) * courant_scale
    courant = scaled * scaled
    older_source, current_source = source_prev, source_now
    older_receiver, current_receiver = recv_prev, recv_now
    image_shots = jnp.zeros(source_now.shape, jnp.float32)
    for moment in range(STEPS):
        new_source = advance(older_source, current_source, courant)
        new_source = deposit(new_source, source_x[:, None], source_yz[:, None], wavelet[:, moment][:, None])
        new_receiver = advance(older_receiver, current_receiver, courant)
        new_receiver = deposit(new_receiver, recv_x, recv_yz, record[:, moment, :])
        image_shots = image_shots + new_source * new_receiver
        older_source, current_source = current_source, new_source
        older_receiver, current_receiver = current_receiver, new_receiver
    image = jnp.zeros((AX, NYS, Z), jnp.float32)
    for member in range(SHOTS):
        placed = lax.dynamic_update_slice_in_dim(jnp.zeros((AX, NYS, Z), jnp.float32), image_shots[member], starts[member // N_PAIR], 1)
        image = image + placed
    return image, current_source, current_receiver
```

```python
import functools

import jax
import jax.numpy as jnp
from jax import lax
from jax.experimental import pallas as pl
from jax.experimental.pallas import tpu as pltpu
from jax.sharding import PartitionSpec as P

STEPS = 6
MESH = pl.DeviceIdType.MESH

stencil_weights = (-205.0 / 72.0, 8.0 / 5.0, -1.0 / 5.0, 8.0 / 315.0, -1.0 / 560.0)
courant_scale = 0.1

PAD = 8
CHUNKS = 2
EARLY, LATE, LATEST = (0, 1, 2), (3,), ()
REACH = 4


def layers_of(d, width):
    return (3 - d, width - 4 + d)


def kernel(
    sizes,
    anchors,
    source_x,
    source_yz,
    wavelet_in,
    recv_x_in,
    recv_yz_in,
    record_in,
    velocity,
    source_prev,
    source_now,
    recv_prev,
    recv_now,
    image_out,
    shot_in,
    source_out,
    recv_out,
    wavelet,
    recv_x,
    recv_yz,
    record,
    field,
    speed,
    courant,
    injected,
    pending,
    stacked,
    mate_out,
    mate_in,
    shot_out,
    image,
    final,
    small_sem,
    load_sem,
    halo_send,
    halo_recv,
    last_send,
    last_recv,
    speed_send,
    speed_recv,
    mate_speed_send,
    mate_speed_recv,
    mate_send,
    mate_recv,
    shot_send,
    shot_recv,
):
    n_tile, n_shot, n_pair = sizes
    width, across, downward = source_now.shape[1:]
    owned = velocity.shape[1]
    survey = owned * n_shot * n_pair
    margin = survey - across
    rows = across // CHUNKS
    tile = lax.axis_index("tile")
    shot = lax.axis_index("shot")
    pair = lax.axis_index("pair")
    mate = 1 - pair
    has_low = tile > 0
    has_high = tile < n_tile - 1
    has = (has_low, has_high)

    def to_shot(k):
        return {"shot": lax.rem(shot + k, n_shot)}

    def to_shot_mate(k):
        return {"shot": lax.rem(shot + k, n_shot), "pair": mate}

    barrier = pltpu.get_barrier_semaphore()

    @pl.when(has_low)
    def _():
        pl.semaphore_signal(barrier, inc=1, device_id={"tile": tile - 1}, device_id_type=MESH)

    @pl.when(has_high)
    def _():
        pl.semaphore_signal(barrier, inc=1, device_id={"tile": tile + 1}, device_id_type=MESH)

    for k in range(1, n_shot):
        pl.semaphore_signal(barrier, inc=1, device_id=to_shot(k), device_id_type=MESH)
        pl.semaphore_signal(barrier, inc=1, device_id=to_shot_mate(k), device_id_type=MESH)
    pl.semaphore_signal(barrier, inc=1, device_id={"pair": mate}, device_id_type=MESH)

    def owner_rows(s, p):
        return pl.ds(pl.multiple_of((s * n_pair + p) * owned, owned), owned)

    inner = pl.ds(PAD, across)
    loads = [
        pltpu.make_async_copy(source_now.at[0], field.at[0, 0, 4 : 4 + width, inner], load_sem.at[0]),
        pltpu.make_async_copy(source_prev.at[0], field.at[1, 0, 4 : 4 + width, inner], load_sem.at[1]),
        pltpu.make_async_copy(recv_now.at[0], field.at[0, 1, 4 : 4 + width, inner], load_sem.at[2]),
        pltpu.make_async_copy(recv_prev.at[0], field.at[1, 1, 4 : 4 + width, inner], load_sem.at[3]),
        pltpu.make_async_copy(velocity, speed.at[:, owner_rows(shot, pair)], load_sem.at[4]),
    ]
    smalls = [
        pltpu.make_async_copy(source, target, small_sem.at[i])
        for i, (source, target) in enumerate(
            (
                (wavelet_in, wavelet),
                (recv_x_in, recv_x),
                (recv_yz_in, recv_yz),
                (record_in, record),
            )
        )
    ]
    for copy in loads + smalls:
        copy.start()

    neighbours = 2 * n_shot - 1 + has_low.astype(jnp.int32) + has_high.astype(jnp.int32)
    pl.semaphore_wait(barrier, neighbours)

    def halo(n, slot, f, c, side):
        landing = pl.ds(pl.multiple_of(PAD + c * rows, 8), rows)
        source, target, other = ((4, 4 + width, tile - 1), (width, 0, tile + 1))[side]
        return pltpu.make_async_remote_copy(
            field.at[slot, f, source : source + 4, landing],
            field.at[slot, f, target : target + 4, landing],
            halo_send.at[lax.rem(n, 2), f, c, side],
            halo_recv.at[lax.rem(n, 2), f, c, 1 - side],
            device_id={"tile": other},
            device_id_type=MESH,
        )

    last_slot = (STEPS - 1) % 2

    def last_halo(d, side):
        source, target, other = ((4 + d, 4 + width + d, tile - 1), (3 + width - d, 3 - d, tile + 1))[side]
        return pltpu.make_async_remote_copy(
            field.at[last_slot, 1, source, inner],
            field.at[last_slot, 1, target, inner],
            last_send.at[d - 1, side] if d else halo_send.at[last_slot, 1, 0, side],
            last_recv.at[d - 1, 1 - side] if d else halo_recv.at[last_slot, 1, 0, 1 - side],
            device_id={"tile": other},
            device_id_type=MESH,
        )

    def last_halos(d):
        for side in range(2):
            @pl.when(has[side])
            def _():
                last_halo(d, side).start()

    def first_halos(f):
        for c in range(CHUNKS):
            for side in range(2):
                @pl.when(has[side])
                def _():
                    halo(0, 0, f, c, side).start()

    loads[0].wait()
    first_halos(0)

    forwarded = ((0, width // 2), (width // 2, width - 1))
    direct = (width - 1, width)

    def speed_copy(k, i):
        first, end = (forwarded + (direct, direct))[i]
        return pltpu.make_async_remote_copy(
            velocity.at[first:end],
            speed.at[first:end, owner_rows(shot, pair)],
            speed_send.at[k - 1, i // 2],
            speed_recv.at[k - 1, i],
            device_id=to_shot_mate(k) if i == 3 else to_shot(k),
            device_id_type=MESH,
        )

    for i in range(2):
        for k in range(1, n_shot):
            speed_copy(k, i).start()
    pltpu.make_async_remote_copy(
        velocity,
        speed.at[:, owner_rows(shot, pair)],
        mate_speed_send.at[0],
        mate_speed_recv.at[0],
        device_id={"pair": mate},
        device_id_type=MESH,
    ).start()

    for slot in range(2):
        for f in range(2):
            field[slot, f, 4 : 4 + width, 0:PAD] = jnp.zeros((width, PAD, downward), jnp.float32)
            field[slot, f, 4 : 4 + width, PAD + across : 2 * PAD + across] = jnp.zeros((width, PAD, downward), jnp.float32)

    def clear(first):
        def body(i, _):
            field[i // 8, (i // 4) % 2, first + i % 4] = jnp.zeros((across + 2 * PAD, downward), jnp.float32)
            return 0

        lax.fori_loop(0, 16, body, 0)

    @pl.when(jnp.logical_not(has_low))
    def _():
        clear(0)

    @pl.when(jnp.logical_not(has_high))
    def _():
        clear(4 + width)

    lane = lax.broadcasted_iota(jnp.int32, (1, 1, downward), 2)
    behind = [jnp.where(lane >= r, stencil_weights[r], 0.0) for r in range(1, 5)]
    ahead = [jnp.where(lane < downward - r, stencil_weights[r], 0.0) for r in range(1, 5)]
    shape = (width, 8, downward)
    local_cell = (
        lax.broadcasted_iota(jnp.int32, shape, 0) * (across * downward)
        + lax.broadcasted_iota(jnp.int32, shape, 1) * downward
        + lax.broadcasted_iota(jnp.int32, shape, 2)
    )
    for copy in smalls:
        copy.wait()
    first = tile * width
    source_cell = (source_x[0] - first) * (across * downward) + source_yz[0]

    place = (recv_x[...] - first) * across + recv_yz[...] // downward
    depth = recv_yz[...] % downward
    receivers = record.shape[2]
    cell = lax.broadcasted_iota(jnp.int32, (width * across, receivers), 0)
    pick = jnp.where(cell == place, 1.0, 0.0).astype(jnp.bfloat16)
    at_depth = lax.broadcasted_iota(jnp.int32, (downward, receivers), 0) == depth

    def inject(n):
        amount = record[n]
        high = amount.astype(jnp.bfloat16).astype(jnp.float32)
        rest = amount - high
        middle = rest.astype(jnp.bfloat16).astype(jnp.float32)
        low = rest - middle
        dense = jnp.zeros((width * across, downward), jnp.float32)
        for piece in (low, middle, high):
            spread = jnp.where(at_depth, piece, 0.0).astype(jnp.bfloat16)
            dense = dense + lax.dot_general(
                pick, spread, (((1,), (1,)), ((), ())), preferred_element_type=jnp.float32
            )
        injected[...] = dense.reshape(width, across, downward)

    def prepare(s, slot, f, y0, imaging):
        at = pl.multiple_of(PAD + y0, 8)
        centre = field[slot, f, 4 : 4 + width, pl.ds(at, 8), :]
        sums = (3.0 * stencil_weights[0]) * centre
        for r in range(1, 5):
            layers = []
            for j in range(width):
                layer = [centre[i : i + 1] for i in (j - r, j + r) if 0 <= i < width]
                layers.append(layer[0] if len(layer) == 1 else layer[0] + layer[1])
            near = jnp.concatenate(layers, axis=0)
            near = near + field[slot, f, 4 : 4 + width, pl.ds(at - r, 8), :]
            near = near + field[slot, f, 4 : 4 + width, pl.ds(at + r, 8), :]
            sums = sums + stencil_weights[r] * near
            sums = sums + behind[r - 1] * pltpu.roll(centre, r, 2)
            sums = sums + ahead[r - 1] * pltpu.roll(centre, downward - r, 2)
        older = field[1 - slot, f, 4 : 4 + width, pl.ds(at, 8), :]
        pending[f, :, pl.ds(y0, 8), :] = sums
        fresh = 2.0 * centre - older
        if f == 0:
            fresh = fresh + jnp.where(local_cell == source_cell - y0 * downward, wavelet[0, s], 0.0)
        else:
            fresh = fresh + injected[:, pl.ds(y0, 8), :]
        field[1 - slot, f, 4 : 4 + width, pl.ds(at, 8), :] = fresh
        if imaging:
            spot = pl.ds(pl.multiple_of(margin + y0, 8), 8)
            stacked[:, spot, :] = stacked[:, spot, :] + centre * field[slot, 0, 4 : 4 + width, pl.ds(at, 8), :]

    def prepare_all(s, f, imaging):
        if f == 1:
            inject(s)

        def ready(t, _):
            prepare(s, lax.rem(s, 2), f, pl.multiple_of(t * 8, 8), imaging)
            return 0

        lax.fori_loop(0, across // 8, ready, 0)

    def outer_low(low, j):
        term = stencil_weights[j + 1] * low[3:4]
        for r in range(j + 2, 5):
            term = term + stencil_weights[r] * low[4 + j - r : 5 + j - r]
        return term

    def outer_high(high, j):
        term = stencil_weights[4 - j] * high[0:1]
        for r in range(5 - j, 5):
            term = term + stencil_weights[r] * high[j - 4 + r : j - 3 + r]
        return term

    def complete(slot, f, y0):
        at = pl.multiple_of(PAD + y0, 8)
        gain = courant[:, pl.ds(y0, 8), :]
        low = field[slot, f, 0:4, pl.ds(at, 8), :]
        high = field[slot, f, 4 + width : 8 + width, pl.ds(at, 8), :]
        middle = [jnp.zeros((width - 8, 8, downward), jnp.float32)] if width > 8 else []
        outer = jnp.concatenate(
            [outer_low(low, j) for j in range(4)] + middle + [outer_high(high, j) for j in range(4)], axis=0
        )
        return field[1 - slot, f, 4 : 4 + width, pl.ds(at, 8), :] + gain * (pending[f, :, pl.ds(y0, 8), :] + outer)

    loads[1].wait()
    prepare_all(0, 0, False)
    loads[2].wait()
    loads[3].wait()
    prepare_all(0, 1, False)
    first_halos(1)
    for i in range(2, 4):
        for k in range(1, n_shot):
            speed_copy(k, i).start()

    def forward(k, i):
        piece_first, piece_end = forwarded[i]
        block = speed.at[piece_first:piece_end, owner_rows(lax.rem(shot + n_shot - k, n_shot), pair)]
        return pltpu.make_async_remote_copy(
            block,
            block,
            mate_speed_send.at[k],
            mate_speed_recv.at[2 * k - 1 + i],
            device_id={"pair": mate},
            device_id_type=MESH,
        )

    for i in range(2):
        for k in range(1, n_shot):
            speed_copy(k, i).wait_recv()
            forward(k, i).start()

    def clear_image(i, _):
        stacked[i] = jnp.zeros((2 * margin + across, downward), jnp.float32)
        return 0

    lax.fori_loop(0, width, clear_image, 0)

    loads[4].wait()
    pltpu.make_async_remote_copy(
        velocity,
        speed.at[:, owner_rows(shot, mate)],
        mate_speed_send.at[0],
        mate_speed_recv.at[0],
        device_id={"pair": mate},
        device_id_type=MESH,
    ).wait()
    for i in range(4):
        for k in range(1, n_shot):
            if i < 2:
                forward(k, i).wait_recv()
            else:
                speed_copy(k, i).wait_recv()
    for k in range(1, n_shot):
        sent = velocity.at[: forwarded[1][1]]
        for together, sem in (
            (sent, speed_send.at[k - 1, 0]),
            (velocity.at[: 2 * (direct[1] - direct[0])], speed_send.at[k - 1, 1]),
            (sent, mate_speed_send.at[k]),
        ):
            pltpu.make_async_copy(together, together, sem).wait()

    start_row = anchors[0]

    def refresh(i, _):
        scaled = speed[i, pl.ds(start_row, across), :] * courant_scale
        courant[i] = scaled * scaled
        return 0

    lax.fori_loop(0, width, refresh, 0)

    def settle(s, f):
        def body(c, _):
            for side in range(2):
                @pl.when(has[side])
                def _():
                    halo(s, lax.rem(s, 2), f, c, side).wait_send()

            return 0

        lax.fori_loop(0, CHUNKS, body, 0)

    def await_halo(s, slot, f, c):
        for side in range(2):
            @pl.when(has[side])
            def _():
                halo(s, slot, f, c, 1 - side).wait_recv()

    def step(s, _):
        slot = lax.rem(s, 2)
        for f in range(2):
            for c in range(CHUNKS):
                await_halo(s, slot, f, c)

                def tiles(t, _):
                    y0 = pl.multiple_of(c * rows + t * 8, 8)
                    field[1 - slot, f, 4 : 4 + width, pl.ds(pl.multiple_of(PAD + y0, 8), 8), :] = complete(slot, f, y0)
                    return 0

                lax.fori_loop(0, rows // 8, tiles, 0)
                for side in range(2):
                    if f == 0:
                        @pl.when(has[side])
                        def _():
                            halo(s + 1, 1 - slot, f, c, side).start()
                    else:
                        @pl.when(jnp.logical_and(has[side], s < STEPS - 2))
                        def _():
                            halo(s + 1, 1 - slot, f, c, side).start()

            if f == 1:
                @pl.when(s == STEPS - 2)
                def _():
                    for d in EARLY:
                        last_halos(d)

            settle(s, f)
            prepare_all(s + 1, f, f == 1)

        return 0

    lax.fori_loop(0, STEPS - 1, step, 0)

    for d in LATE:
        last_halos(d)
    slot = last_slot
    for c in range(CHUNKS):
        await_halo(STEPS - 1, slot, 0, c)

        def tiles(t, _):
            y0 = pl.multiple_of(c * rows + t * 8, 8)
            final[0, :, pl.ds(y0, 8), :] = complete(slot, 0, y0)
            return 0

        lax.fori_loop(0, rows // 8, tiles, 0)

    for d in LATEST:
        last_halos(d)
    source_copy = pltpu.make_async_copy(final.at[0], source_out.at[0], load_sem.at[0])
    source_copy.start()
    spot = pl.ds(margin, across)

    def contribution(s, p, j):
        return stacked[j, pl.ds((s * n_pair + p) * owned + margin - start_row, owned), :]

    def mate_copy(sent, landed, d):
        return pltpu.make_async_remote_copy(
            sent,
            landed,
            mate_send.at[0],
            mate_recv.at[d],
            device_id={"pair": mate},
            device_id_type=MESH,
        )

    def shot_copy(k, d):
        return pltpu.make_async_remote_copy(
            shot_out.at[k - 1, d],
            shot_in.at[k - 1, d],
            shot_send.at[k - 1],
            shot_recv.at[k - 1, d],
            device_id=to_shot(k),
            device_id_type=MESH,
        )

    def finish(d):
        for side in range(2):
            @pl.when(has[side])
            def _():
                last_halo(d, 1 - side).wait_recv()

        low = high = 0.0
        for i in range(d + 1):
            low = low + stencil_weights[4 - d + i] * field[slot, 1, 3 - i, inner, :]
            high = high + stencil_weights[4 - d + i] * field[slot, 1, 4 + width + i, inner, :]
        for j, outer in zip(layers_of(d, width), (low, high)):
            fresh = field[1 - slot, 1, 4 + j, inner, :] + courant[j] * (pending[1, j] + outer)
            final[1, j] = fresh
            stacked[j, spot, :] = stacked[j, spot, :] + fresh * final[0, j]
        for k in list(range(1, n_shot)) + [0]:
            for i, j in enumerate(layers_of(d, width)):
                mate_out[d, k, i] = contribution(lax.rem(shot + k, n_shot), mate, j)
        mate_copy(mate_out.at[d], mate_in.at[d], d).start()

    def hand_over(d):
        mate_copy(mate_out.at[d], mate_in.at[d], d).wait_recv()
        for k in range(1, n_shot):
            for i, j in enumerate(layers_of(d, width)):
                shot_out[k - 1, d, i] = contribution(lax.rem(shot + k, n_shot), pair, j) + mate_in[d, k, i]
            shot_copy(k, d).start()
        for i, j in enumerate(layers_of(d, width)):
            image[j] = contribution(shot, pair, j) + mate_in[d, 0, i]

    finish(0)
    finish(1)
    hand_over(0)
    hand_over(1)
    finish(2)
    hand_over(2)
    finish(3)
    recv_copy = pltpu.make_async_copy(final.at[1], recv_out.at[0], load_sem.at[1])
    recv_copy.start()
    hand_over(3)
    image_copy = pltpu.make_async_copy(image, image_out, load_sem.at[2])
    image_copy.start()
    settle(STEPS - 1, 0)
    for d in range(4):
        for side in range(2):
            @pl.when(has[side])
            def _():
                last_halo(d, side).wait_send()

    mate_copy(mate_out, mate_in, 0).wait_send()
    for k in range(1, n_shot):
        pltpu.make_async_copy(shot_out.at[k - 1], shot_out.at[k - 1], shot_send.at[k - 1]).wait()
    for copy in (source_copy, recv_copy, image_copy):
        copy.wait()
    for d in range(4):
        for k in range(1, n_shot):
            shot_copy(k, d).wait_recv()


def deliver(own, incoming, source, recv, image_out, source_out, recv_out, image, sem):
    width = own.shape[0]
    copies = [
        pltpu.make_async_copy(source, source_out, sem.at[0]),
        pltpu.make_async_copy(recv, recv_out, sem.at[1]),
        pltpu.make_async_copy(image, image_out, sem.at[2]),
    ]
    copies[0].start()
    copies[1].start()
    for d in range(4):
        for i, j in enumerate(layers_of(d, width)):
            total = own[j]
            for k in range(incoming.shape[0]):
                total = total + incoming[k, d, i]
            image[j] = total
    copies[2].start()
    for copy in copies:
        copy.wait()


def solution(mesh):
    sizes = (mesh.shape["tile"], mesh.shape["shot"], mesh.shape["pair"])
    n_shot, n_pair = sizes[1:]

    def shards(velocity, anchors, source_prev, source_now, recv_prev, recv_now, source_x, source_yz, wavelet, recv_x, recv_yz, record):
        width, across, downward = source_now.shape[1:]
        owned = velocity.shape[1]
        survey = owned * n_shot * n_pair
        margin = survey - across
        f32 = jnp.float32
        piece = (4, 2, owned, downward)
        vmem = pl.BlockSpec(memory_space=pltpu.VMEM)
        anywhere = pl.BlockSpec(memory_space=pl.ANY)
        dma = pltpu.SemaphoreType.DMA
        record = jnp.swapaxes(record, 0, 1)
        shapes = (velocity.shape, source_now.shape, recv_now.shape)
        results = pl.pallas_call(
            functools.partial(kernel, sizes),
            out_shape=tuple(pltpu.VMEM(shape, f32) for shape in (shapes[0], (n_shot - 1,) + piece) + shapes[1:]),
            in_specs=[pl.BlockSpec(memory_space=pltpu.SMEM)] * 3 + [anywhere] * 9,
            out_specs=(anywhere,) * 4,
            scratch_shapes=[
                pltpu.SMEM(wavelet.shape, f32),
                pltpu.VMEM(recv_x.shape, jnp.int32),
                pltpu.VMEM(recv_yz.shape, jnp.int32),
                pltpu.VMEM(record.shape, f32),
                pltpu.VMEM((2, 2, width + 8, across + 2 * PAD, downward), f32),
                pltpu.VMEM((width, survey, downward), f32),
                pltpu.VMEM((width, across, downward), f32),
                pltpu.VMEM((width, across, downward), f32),
                pltpu.VMEM((2, width, across, downward), f32),
                pltpu.VMEM((width, across + 2 * margin, downward), f32),
                pltpu.VMEM((4, n_shot) + piece[1:], f32),
                pltpu.VMEM((4, n_shot) + piece[1:], f32),
                pltpu.VMEM((n_shot - 1,) + piece, f32),
                pltpu.VMEM(velocity.shape, f32),
                pltpu.VMEM((2, width, across, downward), f32),
                dma((4,)),
                dma((5,)),
                dma((2, 2, CHUNKS, 2)),
                dma((2, 2, CHUNKS, 2)),
                dma((3, 2)),
                dma((3, 2)),
                dma((n_shot - 1, 2)),
                dma((n_shot - 1, 4)),
                dma((n_shot,)),
                dma((2 * n_shot - 1,)),
                dma((1,)),
                dma((4,)),
                dma((n_shot - 1,)),
                dma((n_shot - 1, 4)),
            ],
            compiler_params=pltpu.CompilerParams(
                collective_id=0, has_side_effects=True, vmem_limit_bytes=40 * 1024 * 1024
            ),
        )(*[
            pltpu.with_memory_space_constraint(operand, pltpu.HBM) if operand.size > 1 else operand
            for operand in (
                anchors, source_x, source_yz, wavelet, recv_x, recv_yz, record,
                velocity, source_prev, source_now, recv_prev, recv_now,
            )
        ])

        return pl.pallas_call(
            deliver,
            out_shape=[jax.ShapeDtypeStruct(shape, f32) for shape in shapes],
            in_specs=[vmem] * 4,
            out_specs=[anywhere] * 3,
            scratch_shapes=[pltpu.VMEM(velocity.shape, f32), dma((3,))],
        )(*[pltpu.with_memory_space_constraint(result, pltpu.VMEM) for result in results])

    in_specs = (
        P(("region", "tile"), ("shot", "pair"), None),
        P(("region", "shot")),
        P(("region", "shot", "pair"), "tile", None, None),
        P(("region", "shot", "pair"), "tile", None, None),
        P(("region", "shot", "pair"), "tile", None, None),
        P(("region", "shot", "pair"), "tile", None, None),
        P(("region", "shot", "pair")),
        P(("region", "shot", "pair")),
        P(("region", "shot", "pair"), None),
        P(("region", "shot", "pair"), None),
        P(("region", "shot", "pair"), None),
        P(("region", "shot", "pair"), None, None),
    )
    out_specs = (
        P(("region", "tile"), ("shot", "pair"), None),
        P(("region", "shot", "pair"), "tile", None, None),
        P(("region", "shot", "pair"), "tile", None, None),
    )
    return jax.shard_map(shards, mesh=mesh, in_specs=in_specs, out_specs=out_specs, check_vma=False)
```

```python
import functools

import jax
import jax.numpy as jnp
from jax import lax
from jax.experimental import pallas as pl
from jax.experimental.pallas import tpu as pltpu
from jax.sharding import PartitionSpec as P

STEPS = 6
MESH = pl.DeviceIdType.MESH

stencil_weights = (-205.0 / 72.0, 8.0 / 5.0, -1.0 / 5.0, 8.0 / 315.0, -1.0 / 560.0)
courant_scale = 0.1

PAD = 8
CHUNKS = 2
AHEAD = 3
REACH = 4


def layers_of(d, width):
    return (3 - d, width - 4 + d)


def kernel(
    sizes,
    anchors,
    source_x,
    source_yz,
    wavelet_in,
    recv_x_in,
    recv_yz_in,
    record_in,
    velocity,
    source_prev,
    source_now,
    recv_prev,
    recv_now,
    image_out,
    shot_in,
    source_out,
    recv_out,
    wavelet,
    recv_x,
    recv_yz,
    record,
    field,
    speed,
    courant,
    injected,
    pending,
    stacked,
    mate_out,
    mate_in,
    shot_out,
    image,
    final,
    small_sem,
    load_sem,
    halo_send,
    halo_recv,
    last_send,
    last_recv,
    speed_send,
    speed_recv,
    mate_speed_send,
    mate_speed_recv,
    mate_send,
    mate_recv,
    shot_send,
    shot_recv,
):
    n_tile, n_shot, n_pair = sizes
    width, across, downward = source_now.shape[1:]
    owned = velocity.shape[1]
    survey = owned * n_shot * n_pair
    margin = survey - across
    rows = across // CHUNKS
    tile = lax.axis_index("tile")
    shot = lax.axis_index("shot")
    pair = lax.axis_index("pair")
    mate = 1 - pair
    has_low = tile > 0
    has_high = tile < n_tile - 1
    has = (has_low, has_high)
    both = jnp.logical_and(has_low, has_high)
    single = jnp.logical_xor(has_low, has_high)

    def to_shot(k):
        return {"shot": lax.rem(shot + k, n_shot)}

    def to_shot_mate(k):
        return {"shot": lax.rem(shot + k, n_shot), "pair": mate}

    barrier = pltpu.get_barrier_semaphore()

    @pl.when(has_low)
    def _():
        pl.semaphore_signal(barrier, inc=1, device_id={"tile": tile - 1}, device_id_type=MESH)

    @pl.when(has_high)
    def _():
        pl.semaphore_signal(barrier, inc=1, device_id={"tile": tile + 1}, device_id_type=MESH)

    for k in range(1, n_shot):
        pl.semaphore_signal(barrier, inc=1, device_id=to_shot(k), device_id_type=MESH)
        pl.semaphore_signal(barrier, inc=1, device_id=to_shot_mate(k), device_id_type=MESH)
    pl.semaphore_signal(barrier, inc=1, device_id={"pair": mate}, device_id_type=MESH)

    def owner_rows(s, p):
        return pl.ds(pl.multiple_of((s * n_pair + p) * owned, owned), owned)

    inner = pl.ds(PAD, across)
    loads = [
        pltpu.make_async_copy(source_now.at[0], field.at[0, 0, 4 : 4 + width, inner], load_sem.at[0]),
        pltpu.make_async_copy(source_prev.at[0], field.at[1, 0, 4 : 4 + width, inner], load_sem.at[1]),
        pltpu.make_async_copy(recv_now.at[0], field.at[0, 1, 4 : 4 + width, inner], load_sem.at[2]),
        pltpu.make_async_copy(recv_prev.at[0], field.at[1, 1, 4 : 4 + width, inner], load_sem.at[3]),
        pltpu.make_async_copy(velocity, speed.at[:, owner_rows(shot, pair)], load_sem.at[4]),
    ]
    smalls = [
        pltpu.make_async_copy(source, target, small_sem.at[i])
        for i, (source, target) in enumerate(
            (
                (wavelet_in, wavelet),
                (recv_x_in, recv_x),
                (recv_yz_in, recv_yz),
                (record_in, record),
            )
        )
    ]
    for copy in loads + smalls:
        copy.start()

    neighbours = 2 * n_shot - 1 + has_low.astype(jnp.int32) + has_high.astype(jnp.int32)
    pl.semaphore_wait(barrier, neighbours)

    def halo(n, slot, f, c, side):
        landing = pl.ds(pl.multiple_of(PAD + c * rows, 8), rows)
        source, target, other = ((4, 4 + width, tile - 1), (width, 0, tile + 1))[side]
        return pltpu.make_async_remote_copy(
            field.at[slot, f, source : source + 4, landing],
            field.at[slot, f, target : target + 4, landing],
            halo_send.at[lax.rem(n, 2), f],
            halo_recv.at[lax.rem(n, 2), f, c],
            device_id={"tile": other},
            device_id_type=MESH,
        )

    last_slot = (STEPS - 1) % 2

    def last_halo(f, d, side):
        source, target, other = ((4 + d, 4 + width + d, tile - 1), (3 + width - d, 3 - d, tile + 1))[side]
        return pltpu.make_async_remote_copy(
            field.at[last_slot, f, source, inner],
            field.at[last_slot, f, target, inner],
            last_send.at[0],
            last_recv.at[d],
            device_id={"tile": other},
            device_id_type=MESH,
        )

    def last_halos(pieces):
        for side in range(2):
            @pl.when(has[side])
            def _():
                for f, d in pieces:
                    last_halo(f, d, side).start()

    def arrived(ref, sem):
        pltpu.make_async_copy(ref, ref, sem).wait()

    def first_halos(f):
        for c in range(CHUNKS):
            for side in range(2):
                @pl.when(has[side])
                def _():
                    halo(0, 0, f, c, side).start()

    forwarded = ((0, width // 2), (width // 2, width - 1))
    direct = (width - 1, width)

    def speed_copy(k, i):
        first, end = (forwarded + (direct, direct))[i]
        return pltpu.make_async_remote_copy(
            velocity.at[first:end],
            speed.at[first:end, owner_rows(shot, pair)],
            speed_send.at[k - 1, i // 2],
            speed_recv.at[k - 1, min(i, 2)],
            device_id=to_shot_mate(k) if i == 3 else to_shot(k),
            device_id_type=MESH,
        )

    for i in range(2):
        for k in range(1, n_shot):
            speed_copy(k, i).start()
    loads[0].wait()
    first_halos(0)
    pltpu.make_async_remote_copy(
        velocity,
        speed.at[:, owner_rows(shot, pair)],
        mate_speed_send.at[0],
        mate_speed_recv.at[0],
        device_id={"pair": mate},
        device_id_type=MESH,
    ).start()

    for slot in range(2):
        for f in range(2):
            field[slot, f, 4 : 4 + width, 0:PAD] = jnp.zeros((width, PAD, downward), jnp.float32)
            field[slot, f, 4 : 4 + width, PAD + across : 2 * PAD + across] = jnp.zeros((width, PAD, downward), jnp.float32)

    def clear(first):
        def body(i, _):
            field[i // 8, (i // 4) % 2, first + i % 4] = jnp.zeros((across + 2 * PAD, downward), jnp.float32)
            return 0

        lax.fori_loop(0, 16, body, 0)

    @pl.when(jnp.logical_not(has_low))
    def _():
        clear(0)

    @pl.when(jnp.logical_not(has_high))
    def _():
        clear(4 + width)

    lane = lax.broadcasted_iota(jnp.int32, (1, 1, downward), 2)
    behind = [jnp.where(lane >= r, stencil_weights[r], 0.0) for r in range(1, 5)]
    ahead = [jnp.where(lane < downward - r, stencil_weights[r], 0.0) for r in range(1, 5)]
    shape = (width, 8, downward)
    local_cell = (
        lax.broadcasted_iota(jnp.int32, shape, 0) * (across * downward)
        + lax.broadcasted_iota(jnp.int32, shape, 1) * downward
        + lax.broadcasted_iota(jnp.int32, shape, 2)
    )
    for copy in smalls:
        copy.wait()
    first = tile * width
    source_cell = (source_x[0] - first) * (across * downward) + source_yz[0]

    place = (recv_x[...] - first) * across + recv_yz[...] // downward
    depth = recv_yz[...] % downward
    receivers = record.shape[2]
    cell = lax.broadcasted_iota(jnp.int32, (width * across, receivers), 0)
    pick = jnp.where(cell == place, 1.0, 0.0).astype(jnp.bfloat16)
    at_depth = lax.broadcasted_iota(jnp.int32, (downward, receivers), 0) == depth

    def inject(n):
        amount = record[n]
        high = amount.astype(jnp.bfloat16).astype(jnp.float32)
        rest = amount - high
        middle = rest.astype(jnp.bfloat16).astype(jnp.float32)
        low = rest - middle
        dense = jnp.zeros((width * across, downward), jnp.float32)
        for piece in (low, middle, high):
            spread = jnp.where(at_depth, piece, 0.0).astype(jnp.bfloat16)
            dense = dense + lax.dot_general(
                pick, spread, (((1,), (1,)), ((), ())), preferred_element_type=jnp.float32
            )
        injected[...] = dense.reshape(width, across, downward)

    def prepare(s, slot, f, y0, imaging):
        at = pl.multiple_of(PAD + y0, 8)
        centre = field[slot, f, 4 : 4 + width, pl.ds(at, 8), :]
        sums = (3.0 * stencil_weights[0]) * centre
        for r in range(1, 5):
            layers = []
            for j in range(width):
                layer = [centre[i : i + 1] for i in (j - r, j + r) if 0 <= i < width]
                layers.append(layer[0] if len(layer) == 1 else layer[0] + layer[1])
            near = jnp.concatenate(layers, axis=0)
            near = near + field[slot, f, 4 : 4 + width, pl.ds(at - r, 8), :]
            near = near + field[slot, f, 4 : 4 + width, pl.ds(at + r, 8), :]
            sums = sums + stencil_weights[r] * near
            sums = sums + behind[r - 1] * pltpu.roll(centre, r, 2)
            sums = sums + ahead[r - 1] * pltpu.roll(centre, downward - r, 2)
        older = field[1 - slot, f, 4 : 4 + width, pl.ds(at, 8), :]
        pending[f, :, pl.ds(y0, 8), :] = sums
        fresh = 2.0 * centre - older
        if f == 0:
            fresh = fresh + jnp.where(local_cell == source_cell - y0 * downward, wavelet[0, s], 0.0)
        else:
            fresh = fresh + injected[:, pl.ds(y0, 8), :]
        field[1 - slot, f, 4 : 4 + width, pl.ds(at, 8), :] = fresh
        if imaging:
            spot = pl.ds(pl.multiple_of(margin + y0, 8), 8)
            stacked[:, spot, :] = stacked[:, spot, :] + centre * field[slot, 0, 4 : 4 + width, pl.ds(at, 8), :]

    def prepare_all(s, f, imaging):
        if f == 1:
            inject(s)

        def ready(t, _):
            prepare(s, lax.rem(s, 2), f, pl.multiple_of(t * 8, 8), imaging)
            return 0

        lax.fori_loop(0, across // 8, ready, 0)

    def outer_low(low, j):
        term = stencil_weights[j + 1] * low[3:4]
        for r in range(j + 2, 5):
            term = term + stencil_weights[r] * low[4 + j - r : 5 + j - r]
        return term

    def outer_high(high, j):
        term = stencil_weights[4 - j] * high[0:1]
        for r in range(5 - j, 5):
            term = term + stencil_weights[r] * high[j - 4 + r : j - 3 + r]
        return term

    def complete(slot, f, y0):
        at = pl.multiple_of(PAD + y0, 8)
        gain = courant[:, pl.ds(y0, 8), :]
        low = field[slot, f, 0:4, pl.ds(at, 8), :]
        high = field[slot, f, 4 + width : 8 + width, pl.ds(at, 8), :]
        middle = [jnp.zeros((width - 8, 8, downward), jnp.float32)] if width > 8 else []
        outer = jnp.concatenate(
            [outer_low(low, j) for j in range(4)] + middle + [outer_high(high, j) for j in range(4)], axis=0
        )
        return field[1 - slot, f, 4 : 4 + width, pl.ds(at, 8), :] + gain * (pending[f, :, pl.ds(y0, 8), :] + outer)

    loads[1].wait()
    prepare_all(0, 0, False)
    loads[2].wait()
    loads[3].wait()
    prepare_all(0, 1, False)
    first_halos(1)
    for i in range(2, 4):
        for k in range(1, n_shot):
            speed_copy(k, i).start()

    def forward(k, i):
        piece_first, piece_end = forwarded[i]
        block = speed.at[piece_first:piece_end, owner_rows(lax.rem(shot + n_shot - k, n_shot), pair)]
        return pltpu.make_async_remote_copy(
            block,
            block,
            mate_speed_send.at[k],
            mate_speed_recv.at[k],
            device_id={"pair": mate},
            device_id_type=MESH,
        )

    for i in range(2):
        for k in range(1, n_shot):
            speed_copy(k, i).wait_recv()
            forward(k, i).start()

    def clear_image(i, _):
        stacked[i] = jnp.zeros((2 * margin + across, downward), jnp.float32)
        return 0

    lax.fori_loop(0, width, clear_image, 0)

    loads[4].wait()
    pltpu.make_async_remote_copy(
        velocity,
        speed.at[:, owner_rows(shot, mate)],
        mate_speed_send.at[0],
        mate_speed_recv.at[0],
        device_id={"pair": mate},
        device_id_type=MESH,
    ).wait()
    sent = velocity.at[: forwarded[1][1]]
    twice = velocity.at[: 2 * (direct[1] - direct[0])]
    for k in range(1, n_shot):
        arrived(sent, mate_speed_recv.at[k])
        arrived(twice, speed_recv.at[k - 1, 2])
        arrived(sent, speed_send.at[k - 1, 0])
        arrived(twice, speed_send.at[k - 1, 1])
        arrived(sent, mate_speed_send.at[k])

    start_row = anchors[0]

    def refresh(i, _):
        scaled = speed[i, pl.ds(start_row, across), :] * courant_scale
        courant[i] = scaled * scaled
        return 0

    lax.fori_loop(0, width, refresh, 0)

    def settle(s, f):
        @pl.when(both)
        def _():
            arrived(field.at[0, f, 4:12, inner], halo_send.at[lax.rem(s, 2), f])

        @pl.when(single)
        def _():
            arrived(field.at[0, f, 4:8, inner], halo_send.at[lax.rem(s, 2), f])

    def await_halo(s, slot, f, c):
        landing = pl.ds(PAD + c * rows, rows)

        @pl.when(both)
        def _():
            arrived(field.at[slot, f, 4:12, landing], halo_recv.at[lax.rem(s, 2), f, c])

        @pl.when(single)
        def _():
            arrived(field.at[slot, f, 4:8, landing], halo_recv.at[lax.rem(s, 2), f, c])

    def step(s, _):
        slot = lax.rem(s, 2)
        for f in range(2):
            for c in range(CHUNKS):
                await_halo(s, slot, f, c)

                def tiles(t, _):
                    y0 = pl.multiple_of(c * rows + t * 8, 8)
                    field[1 - slot, f, 4 : 4 + width, pl.ds(pl.multiple_of(PAD + y0, 8), 8), :] = complete(slot, f, y0)
                    return 0

                lax.fori_loop(0, rows // 8, tiles, 0)
                for side in range(2):
                    @pl.when(jnp.logical_and(has[side], s < STEPS - 2))
                    def _():
                        halo(s + 1, 1 - slot, f, c, side).start()

            @pl.when(s == STEPS - 2)
            def _():
                if f == 0:
                    last_halos([(0, d) for d in range(AHEAD)])
                else:
                    last_halos([(1, d) for d in range(AHEAD - 1)])
                    for d in range(AHEAD - 1, 4):
                        last_halos([(e, d) for e in range(2) if e or d >= AHEAD])

            settle(s, f)
            prepare_all(s + 1, f, f == 1)

        return 0

    lax.fori_loop(0, STEPS - 1, step, 0)

    slot = last_slot
    spot = pl.ds(margin, across)

    def contribution(s, p, j):
        return stacked[j, pl.ds((s * n_pair + p) * owned + margin - start_row, owned), :]

    def mate_copy(blocks, d):
        return pltpu.make_async_remote_copy(
            mate_out.at[d, :blocks],
            mate_in.at[d, :blocks],
            mate_send.at[0],
            mate_recv.at[d],
            device_id={"pair": mate},
            device_id_type=MESH,
        )

    def shot_copy(k, p, d):
        return pltpu.make_async_remote_copy(
            shot_out.at[k - 1, p, d],
            shot_in.at[k - 1, d],
            shot_send.at[k - 1],
            shot_recv.at[k - 1],
            device_id={"shot": lax.rem(shot + k, n_shot), "pair": p},
            device_id_type=MESH,
        )

    given = [(k, p) for k in range(1, n_shot) for p in range(n_pair)] + [(0, 0)]

    def finish(d):
        @pl.when(both)
        def _():
            arrived(field.at[slot, :, 4:6, inner], last_recv.at[d])

        @pl.when(single)
        def _():
            arrived(field.at[slot, :, 4:5, inner], last_recv.at[d])

        for side, j in enumerate(layers_of(d, width)):
            fresh = []
            for f in range(2):
                outer = 0.0
                for i in range(d + 1):
                    ghost = 4 + width + i if side else 3 - i
                    outer = outer + stencil_weights[4 - d + i] * field[slot, f, ghost, inner, :]
                fresh.append(field[1 - slot, f, 4 + j, inner, :] + courant[j] * (pending[f, j] + outer))
                final[f, j] = fresh[f]
            stacked[j, spot, :] = stacked[j, spot, :] + fresh[0] * fresh[1]

    def give(d):
        for b, (k, p) in enumerate(given):
            for i, j in enumerate(layers_of(d, width)):
                mate_out[d, b, i] = contribution(lax.rem(shot + k, n_shot), p, j)
        mate_copy(len(given), d).start()

    def gather(d):
        mate_copy(len(given), d).wait_recv()
        for b, (k, p) in enumerate(given):
            for i, j in enumerate(layers_of(d, width)):
                total = contribution(lax.rem(shot + k, n_shot), p, j) + mate_in[d, b, i]
                if k:
                    shot_out[k - 1, p, d, i] = total
                else:
                    image[j] = total
            if k:
                shot_copy(k, p, d).start()
        for i, j in enumerate(layers_of(d, width)):
            mate_out[d, 0, i] = contribution(shot, 1, j)
        mate_copy(1, d).start()

    def keep(d):
        mate_copy(1, d).wait_recv()
        for i, j in enumerate(layers_of(d, width)):
            image[j] = contribution(shot, 1, j) + mate_in[d, 0, i]

    source_copy = pltpu.make_async_copy(final.at[0], source_out.at[0], load_sem.at[0])
    recv_copy = pltpu.make_async_copy(final.at[1], recv_out.at[0], load_sem.at[1])
    image_copy = pltpu.make_async_copy(image, image_out, load_sem.at[2])

    @pl.when(pair == 0)
    def _():
        for d in range(4):
            finish(d)
            gather(d)
        image_copy.start()
        source_copy.start()
        recv_copy.start()
        arrived(mate_out.at[:, 0], mate_send.at[0])
        for k in range(1, n_shot):
            arrived(shot_out.at[k - 1], shot_send.at[k - 1])

    @pl.when(pair == 1)
    def _():
        for d in range(4):
            finish(d)
            give(d)
        source_copy.start()
        recv_copy.start()
        for d in range(4):
            keep(d)
        image_copy.start()
        arrived(mate_out, mate_send.at[0])

    @pl.when(both)
    def _():
        arrived(field.at[slot, :, 4:12, inner], last_send.at[0])

    @pl.when(single)
    def _():
        arrived(field.at[slot, :, 4:8, inner], last_send.at[0])

    for copy in (source_copy, recv_copy, image_copy):
        copy.wait()
    for k in range(1, n_shot):
        arrived(shot_in.at[k - 1], shot_recv.at[k - 1])


def deliver(own, incoming, source, recv, image_out, source_out, recv_out, image, sem):
    width = own.shape[0]
    copies = [
        pltpu.make_async_copy(source, source_out, sem.at[0]),
        pltpu.make_async_copy(recv, recv_out, sem.at[1]),
        pltpu.make_async_copy(image, image_out, sem.at[2]),
    ]
    copies[0].start()
    copies[1].start()
    for d in range(4):
        for i, j in enumerate(layers_of(d, width)):
            total = own[j]
            for k in range(incoming.shape[0]):
                total = total + incoming[k, d, i]
            image[j] = total
    copies[2].start()
    for copy in copies:
        copy.wait()


def solution(mesh):
    sizes = (mesh.shape["tile"], mesh.shape["shot"], mesh.shape["pair"])
    n_shot, n_pair = sizes[1:]

    def shards(velocity, anchors, source_prev, source_now, recv_prev, recv_now, source_x, source_yz, wavelet, recv_x, recv_yz, record):
        width, across, downward = source_now.shape[1:]
        owned = velocity.shape[1]
        survey = owned * n_shot * n_pair
        margin = survey - across
        f32 = jnp.float32
        piece = (4, 2, owned, downward)
        vmem = pl.BlockSpec(memory_space=pltpu.VMEM)
        anywhere = pl.BlockSpec(memory_space=pl.ANY)
        dma = pltpu.SemaphoreType.DMA
        record = jnp.swapaxes(record, 0, 1)
        shapes = (velocity.shape, source_now.shape, recv_now.shape)
        results = pl.pallas_call(
            functools.partial(kernel, sizes),
            out_shape=tuple(pltpu.VMEM(shape, f32) for shape in (shapes[0], (n_shot - 1,) + piece) + shapes[1:]),
            in_specs=[pl.BlockSpec(memory_space=pltpu.SMEM)] * 3 + [anywhere] * 9,
            out_specs=(anywhere,) * 4,
            scratch_shapes=[
                pltpu.SMEM(wavelet.shape, f32),
                pltpu.VMEM(recv_x.shape, jnp.int32),
                pltpu.VMEM(recv_yz.shape, jnp.int32),
                pltpu.VMEM(record.shape, f32),
                pltpu.VMEM((2, 2, width + 8, across + 2 * PAD, downward), f32),
                pltpu.VMEM((width, survey, downward), f32),
                pltpu.VMEM((width, across, downward), f32),
                pltpu.VMEM((width, across, downward), f32),
                pltpu.VMEM((2, width, across, downward), f32),
                pltpu.VMEM((width, across + 2 * margin, downward), f32),
                pltpu.VMEM((4, 2 * n_shot - 1) + piece[1:], f32),
                pltpu.VMEM((4, 2 * n_shot - 1) + piece[1:], f32),
                pltpu.VMEM((n_shot - 1, n_pair) + piece, f32),
                pltpu.VMEM(velocity.shape, f32),
                pltpu.VMEM((2, width, across, downward), f32),
                dma((4,)),
                dma((5,)),
                dma((2, 2)),
                dma((2, 2, CHUNKS)),
                dma((1,)),
                dma((4,)),
                dma((n_shot - 1, 2)),
                dma((n_shot - 1, 3)),
                dma((n_shot,)),
                dma((n_shot,)),
                dma((1,)),
                dma((4,)),
                dma((n_shot - 1,)),
                dma((n_shot - 1,)),
            ],
            compiler_params=pltpu.CompilerParams(
                collective_id=0, has_side_effects=True, vmem_limit_bytes=40 * 1024 * 1024
            ),
        )(*[
            pltpu.with_memory_space_constraint(operand, pltpu.HBM) if operand.size > 1 else operand
            for operand in (
                anchors, source_x, source_yz, wavelet, recv_x, recv_yz, record,
                velocity, source_prev, source_now, recv_prev, recv_now,
            )
        ])

        return pl.pallas_call(
            deliver,
            out_shape=[jax.ShapeDtypeStruct(shape, f32) for shape in shapes],
            in_specs=[vmem] * 4,
            out_specs=[anywhere] * 3,
            scratch_shapes=[pltpu.VMEM(velocity.shape, f32), dma((3,))],
        )(*[pltpu.with_memory_space_constraint(result, pltpu.VMEM) for result in results])

    in_specs = (
        P(("region", "tile"), ("shot", "pair"), None),
        P(("region", "shot")),
        P(("region", "shot", "pair"), "tile", None, None),
        P(("region", "shot", "pair"), "tile", None, None),
        P(("region", "shot", "pair"), "tile", None, None),
        P(("region", "shot", "pair"), "tile", None, None),
        P(("region", "shot", "pair")),
        P(("region", "shot", "pair")),
        P(("region", "shot", "pair"), None),
        P(("region", "shot", "pair"), None),
        P(("region", "shot", "pair"), None),
        P(("region", "shot", "pair"), None, None),
    )
    out_specs = (
        P(("region", "tile"), ("shot", "pair"), None),
        P(("region", "shot", "pair"), "tile", None, None),
        P(("region", "shot", "pair"), "tile", None, None),
    )
    return jax.shard_map(shards, mesh=mesh, in_specs=in_specs, out_specs=out_specs, check_vma=False)
```

```python
import functools

import jax
import jax.numpy as jnp
from jax import lax
from jax.experimental import pallas as pl
from jax.experimental.pallas import tpu as pltpu
from jax.sharding import PartitionSpec as P

STEPS = 6
MESH = pl.DeviceIdType.MESH

stencil_weights = (-205.0 / 72.0, 8.0 / 5.0, -1.0 / 5.0, 8.0 / 315.0, -1.0 / 560.0)
courant_scale = 0.1

PAD = 8
CHUNKS = 2
AHEAD = 3
SOON = 2
ORDER = ((1, 2), (0, 3), (1, 3))
REACH = 4


def layers_of(d, width):
    return (3 - d, width - 4 + d)


def kernel(
    sizes,
    anchors,
    source_x,
    source_yz,
    wavelet_in,
    recv_x_in,
    recv_yz_in,
    record_in,
    velocity,
    source_prev,
    source_now,
    recv_prev,
    recv_now,
    image_out,
    shot_in,
    source_out,
    recv_out,
    wavelet,
    recv_x,
    recv_yz,
    record,
    field,
    speed,
    courant,
    injected,
    pending,
    stacked,
    mate_out,
    mate_in,
    shot_out,
    image,
    final,
    small_sem,
    load_sem,
    halo_send,
    halo_recv,
    last_send,
    last_recv,
    speed_send,
    speed_recv,
    mate_speed_send,
    mate_speed_recv,
    mate_send,
    mate_recv,
    shot_send,
    shot_recv,
):
    n_tile, n_shot, n_pair = sizes
    width, across, downward = source_now.shape[1:]
    owned = velocity.shape[1]
    survey = owned * n_shot * n_pair
    margin = survey - across
    rows = across // CHUNKS
    tile = lax.axis_index("tile")
    shot = lax.axis_index("shot")
    pair = lax.axis_index("pair")
    mate = 1 - pair
    has_low = tile > 0
    has_high = tile < n_tile - 1
    has = (has_low, has_high)
    both = jnp.logical_and(has_low, has_high)
    single = jnp.logical_xor(has_low, has_high)

    def to_shot(k):
        return {"shot": lax.rem(shot + k, n_shot)}

    def to_shot_mate(k):
        return {"shot": lax.rem(shot + k, n_shot), "pair": mate}

    barrier = pltpu.get_barrier_semaphore()

    @pl.when(has_low)
    def _():
        pl.semaphore_signal(barrier, inc=1, device_id={"tile": tile - 1}, device_id_type=MESH)

    @pl.when(has_high)
    def _():
        pl.semaphore_signal(barrier, inc=1, device_id={"tile": tile + 1}, device_id_type=MESH)

    for k in range(1, n_shot):
        pl.semaphore_signal(barrier, inc=1, device_id=to_shot(k), device_id_type=MESH)
        pl.semaphore_signal(barrier, inc=1, device_id=to_shot_mate(k), device_id_type=MESH)
    pl.semaphore_signal(barrier, inc=1, device_id={"pair": mate}, device_id_type=MESH)

    def owner_rows(s, p):
        return pl.ds(pl.multiple_of((s * n_pair + p) * owned, owned), owned)

    inner = pl.ds(PAD, across)
    loads = [
        pltpu.make_async_copy(source_now.at[0], field.at[0, 0, 4 : 4 + width, inner], load_sem.at[0]),
        pltpu.make_async_copy(source_prev.at[0], field.at[1, 0, 4 : 4 + width, inner], load_sem.at[1]),
        pltpu.make_async_copy(recv_now.at[0], field.at[0, 1, 4 : 4 + width, inner], load_sem.at[2]),
        pltpu.make_async_copy(recv_prev.at[0], field.at[1, 1, 4 : 4 + width, inner], load_sem.at[3]),
        pltpu.make_async_copy(velocity, speed.at[:, owner_rows(shot, pair)], load_sem.at[4]),
    ]
    smalls = [
        pltpu.make_async_copy(source, target, small_sem.at[i])
        for i, (source, target) in enumerate(
            (
                (wavelet_in, wavelet),
                (recv_x_in, recv_x),
                (recv_yz_in, recv_yz),
                (record_in, record),
            )
        )
    ]
    for copy in loads + smalls:
        copy.start()

    neighbours = 2 * n_shot - 1 + has_low.astype(jnp.int32) + has_high.astype(jnp.int32)
    pl.semaphore_wait(barrier, neighbours)

    def halo(n, slot, f, c, side):
        landing = pl.ds(pl.multiple_of(PAD + c * rows, 8), rows)
        source, target, other = ((4, 4 + width, tile - 1), (width, 0, tile + 1))[side]
        return pltpu.make_async_remote_copy(
            field.at[slot, f, source : source + 4, landing],
            field.at[slot, f, target : target + 4, landing],
            halo_send.at[lax.rem(n, 2), f],
            halo_recv.at[lax.rem(n, 2), f, c],
            device_id={"tile": other},
            device_id_type=MESH,
        )

    last_slot = (STEPS - 1) % 2

    def last_halo(f, d, part, side):
        landing = inner if part is None else pl.ds(PAD + part * rows, rows)
        source, target, other = ((4 + d, 4 + width + d, tile - 1), (3 + width - d, 3 - d, tile + 1))[side]
        return pltpu.make_async_remote_copy(
            field.at[last_slot, f, source, landing],
            field.at[last_slot, f, target, landing],
            last_send.at[0],
            last_recv.at[d],
            device_id={"tile": other},
            device_id_type=MESH,
        )

    def last_halos(pieces):
        for side in range(2):
            @pl.when(has[side])
            def _():
                for f, d, part in pieces:
                    last_halo(f, d, part, side).start()

    def arrived(ref, sem):
        pltpu.make_async_copy(ref, ref, sem).wait()

    def first_halos(f):
        for c in range(CHUNKS):
            for side in range(2):
                @pl.when(has[side])
                def _():
                    halo(0, 0, f, c, side).start()

    forwarded = ((0, width // 2), (width // 2, width - 1))
    direct = (width - 1, width)

    def speed_copy(k, i):
        first, end = (forwarded + (direct, direct))[i]
        return pltpu.make_async_remote_copy(
            velocity.at[first:end],
            speed.at[first:end, owner_rows(shot, pair)],
            speed_send.at[k - 1, i // 2],
            speed_recv.at[k - 1, min(i, 2)],
            device_id=to_shot_mate(k) if i == 3 else to_shot(k),
            device_id_type=MESH,
        )

    for i in range(2):
        for k in range(1, n_shot):
            speed_copy(k, i).start()
    loads[0].wait()
    first_halos(0)
    pltpu.make_async_remote_copy(
        velocity,
        speed.at[:, owner_rows(shot, pair)],
        mate_speed_send.at[0],
        mate_speed_recv.at[0],
        device_id={"pair": mate},
        device_id_type=MESH,
    ).start()

    for slot in range(2):
        for f in range(2):
            field[slot, f, 4 : 4 + width, 0:PAD] = jnp.zeros((width, PAD, downward), jnp.float32)
            field[slot, f, 4 : 4 + width, PAD + across : 2 * PAD + across] = jnp.zeros((width, PAD, downward), jnp.float32)

    def clear(first):
        def body(i, _):
            field[i // 8, (i // 4) % 2, first + i % 4] = jnp.zeros((across + 2 * PAD, downward), jnp.float32)
            return 0

        lax.fori_loop(0, 16, body, 0)

    @pl.when(jnp.logical_not(has_low))
    def _():
        clear(0)

    @pl.when(jnp.logical_not(has_high))
    def _():
        clear(4 + width)

    lane = lax.broadcasted_iota(jnp.int32, (1, 1, downward), 2)
    behind = [jnp.where(lane >= r, stencil_weights[r], 0.0) for r in range(1, 5)]
    ahead = [jnp.where(lane < downward - r, stencil_weights[r], 0.0) for r in range(1, 5)]
    shape = (width, 8, downward)
    local_cell = (
        lax.broadcasted_iota(jnp.int32, shape, 0) * (across * downward)
        + lax.broadcasted_iota(jnp.int32, shape, 1) * downward
        + lax.broadcasted_iota(jnp.int32, shape, 2)
    )
    for copy in smalls:
        copy.wait()
    first = tile * width
    source_cell = (source_x[0] - first) * (across * downward) + source_yz[0]

    place = (recv_x[...] - first) * across + recv_yz[...] // downward
    depth = recv_yz[...] % downward
    receivers = record.shape[2]
    cell = lax.broadcasted_iota(jnp.int32, (width * across, receivers), 0)
    pick = jnp.where(cell == place, 1.0, 0.0).astype(jnp.bfloat16)
    at_depth = lax.broadcasted_iota(jnp.int32, (downward, receivers), 0) == depth

    def inject(n):
        amount = record[n]
        high = amount.astype(jnp.bfloat16).astype(jnp.float32)
        rest = amount - high
        middle = rest.astype(jnp.bfloat16).astype(jnp.float32)
        low = rest - middle
        dense = jnp.zeros((width * across, downward), jnp.float32)
        for piece in (low, middle, high):
            spread = jnp.where(at_depth, piece, 0.0).astype(jnp.bfloat16)
            dense = dense + lax.dot_general(
                pick, spread, (((1,), (1,)), ((), ())), preferred_element_type=jnp.float32
            )
        injected[...] = dense.reshape(width, across, downward)

    def prepare(s, slot, f, y0, imaging):
        at = pl.multiple_of(PAD + y0, 8)
        centre = field[slot, f, 4 : 4 + width, pl.ds(at, 8), :]
        sums = (3.0 * stencil_weights[0]) * centre
        for r in range(1, 5):
            layers = []
            for j in range(width):
                layer = [centre[i : i + 1] for i in (j - r, j + r) if 0 <= i < width]
                layers.append(layer[0] if len(layer) == 1 else layer[0] + layer[1])
            near = jnp.concatenate(layers, axis=0)
            near = near + field[slot, f, 4 : 4 + width, pl.ds(at - r, 8), :]
            near = near + field[slot, f, 4 : 4 + width, pl.ds(at + r, 8), :]
            sums = sums + stencil_weights[r] * near
            sums = sums + behind[r - 1] * pltpu.roll(centre, r, 2)
            sums = sums + ahead[r - 1] * pltpu.roll(centre, downward - r, 2)
        older = field[1 - slot, f, 4 : 4 + width, pl.ds(at, 8), :]
        pending[f, :, pl.ds(y0, 8), :] = sums
        fresh = 2.0 * centre - older
        if f == 0:
            fresh = fresh + jnp.where(local_cell == source_cell - y0 * downward, wavelet[0, s], 0.0)
        else:
            fresh = fresh + injected[:, pl.ds(y0, 8), :]
        field[1 - slot, f, 4 : 4 + width, pl.ds(at, 8), :] = fresh
        if imaging:
            spot = pl.ds(pl.multiple_of(margin + y0, 8), 8)
            stacked[:, spot, :] = stacked[:, spot, :] + centre * field[slot, 0, 4 : 4 + width, pl.ds(at, 8), :]

    def prepare_all(s, f, imaging):
        if f == 1:
            inject(s)

        def ready(t, _):
            prepare(s, lax.rem(s, 2), f, pl.multiple_of(t * 8, 8), imaging)
            return 0

        lax.fori_loop(0, across // 8, ready, 0)

    def outer_low(low, j):
        term = stencil_weights[j + 1] * low[3:4]
        for r in range(j + 2, 5):
            term = term + stencil_weights[r] * low[4 + j - r : 5 + j - r]
        return term

    def outer_high(high, j):
        term = stencil_weights[4 - j] * high[0:1]
        for r in range(5 - j, 5):
            term = term + stencil_weights[r] * high[j - 4 + r : j - 3 + r]
        return term

    def complete(slot, f, y0):
        at = pl.multiple_of(PAD + y0, 8)
        gain = courant[:, pl.ds(y0, 8), :]
        low = field[slot, f, 0:4, pl.ds(at, 8), :]
        high = field[slot, f, 4 + width : 8 + width, pl.ds(at, 8), :]
        middle = [jnp.zeros((width - 8, 8, downward), jnp.float32)] if width > 8 else []
        outer = jnp.concatenate(
            [outer_low(low, j) for j in range(4)] + middle + [outer_high(high, j) for j in range(4)], axis=0
        )
        return field[1 - slot, f, 4 : 4 + width, pl.ds(at, 8), :] + gain * (pending[f, :, pl.ds(y0, 8), :] + outer)

    loads[1].wait()
    prepare_all(0, 0, False)
    loads[2].wait()
    loads[3].wait()
    prepare_all(0, 1, False)
    first_halos(1)
    for i in range(2, 4):
        for k in range(1, n_shot):
            speed_copy(k, i).start()

    def forward(k, i):
        piece_first, piece_end = forwarded[i]
        block = speed.at[piece_first:piece_end, owner_rows(lax.rem(shot + n_shot - k, n_shot), pair)]
        return pltpu.make_async_remote_copy(
            block,
            block,
            mate_speed_send.at[k],
            mate_speed_recv.at[k],
            device_id={"pair": mate},
            device_id_type=MESH,
        )

    for i in range(2):
        for k in range(1, n_shot):
            speed_copy(k, i).wait_recv()
            forward(k, i).start()

    def clear_image(i, _):
        stacked[i] = jnp.zeros((2 * margin + across, downward), jnp.float32)
        return 0

    lax.fori_loop(0, width, clear_image, 0)

    loads[4].wait()
    pltpu.make_async_remote_copy(
        velocity,
        speed.at[:, owner_rows(shot, mate)],
        mate_speed_send.at[0],
        mate_speed_recv.at[0],
        device_id={"pair": mate},
        device_id_type=MESH,
    ).wait()
    sent = velocity.at[: forwarded[1][1]]
    twice = velocity.at[: 2 * (direct[1] - direct[0])]
    for k in range(1, n_shot):
        arrived(sent, mate_speed_recv.at[k])
        arrived(twice, speed_recv.at[k - 1, 2])
        arrived(sent, speed_send.at[k - 1, 0])
        arrived(twice, speed_send.at[k - 1, 1])
        arrived(sent, mate_speed_send.at[k])

    start_row = anchors[0]

    def refresh(i, _):
        scaled = speed[i, pl.ds(start_row, across), :] * courant_scale
        courant[i] = scaled * scaled
        return 0

    lax.fori_loop(0, width, refresh, 0)

    def settle(s, f):
        @pl.when(both)
        def _():
            arrived(field.at[0, f, 4:12, inner], halo_send.at[lax.rem(s, 2), f])

        @pl.when(single)
        def _():
            arrived(field.at[0, f, 4:8, inner], halo_send.at[lax.rem(s, 2), f])

    def await_halo(s, slot, f, c):
        landing = pl.ds(PAD + c * rows, rows)

        @pl.when(both)
        def _():
            arrived(field.at[slot, f, 4:12, landing], halo_recv.at[lax.rem(s, 2), f, c])

        @pl.when(single)
        def _():
            arrived(field.at[slot, f, 4:8, landing], halo_recv.at[lax.rem(s, 2), f, c])

    def step(s, _):
        slot = lax.rem(s, 2)
        for f in range(2):
            for c in range(CHUNKS):
                await_halo(s, slot, f, c)

                def tiles(t, _):
                    y0 = pl.multiple_of(c * rows + t * 8, 8)
                    field[1 - slot, f, 4 : 4 + width, pl.ds(pl.multiple_of(PAD + y0, 8), 8), :] = complete(slot, f, y0)
                    return 0

                lax.fori_loop(0, rows // 8, tiles, 0)
                for side in range(2):
                    @pl.when(jnp.logical_and(has[side], s < STEPS - 2))
                    def _():
                        halo(s + 1, 1 - slot, f, c, side).start()

                if f == 1:
                    @pl.when(s == STEPS - 2)
                    def _():
                        last_halos([(1, d, c) for d in range(SOON)])
                        if c == CHUNKS - 1:
                            last_halos([(e, d, None) for e, d in ORDER])

            if f == 0:
                @pl.when(s == STEPS - 2)
                def _():
                    last_halos([(0, d, None) for d in range(AHEAD)])

            settle(s, f)
            prepare_all(s + 1, f, f == 1)

        return 0

    lax.fori_loop(0, STEPS - 1, step, 0)

    slot = last_slot
    spot = pl.ds(margin, across)

    def contribution(s, p, j):
        return stacked[j, pl.ds((s * n_pair + p) * owned + margin - start_row, owned), :]

    def mate_copy(blocks, d):
        return pltpu.make_async_remote_copy(
            mate_out.at[d, :blocks],
            mate_in.at[d, :blocks],
            mate_send.at[0],
            mate_recv.at[d],
            device_id={"pair": mate},
            device_id_type=MESH,
        )

    def shot_copy(k, p, d):
        return pltpu.make_async_remote_copy(
            shot_out.at[k - 1, p, d],
            shot_in.at[k - 1, d],
            shot_send.at[k - 1],
            shot_recv.at[k - 1],
            device_id={"shot": lax.rem(shot + k, n_shot), "pair": p},
            device_id_type=MESH,
        )

    given = [(k, p) for k in range(1, n_shot) for p in range(n_pair)] + [(0, 0)]

    def finish(d):
        @pl.when(both)
        def _():
            arrived(field.at[slot, :, 4:6, inner], last_recv.at[d])

        @pl.when(single)
        def _():
            arrived(field.at[slot, :, 4:5, inner], last_recv.at[d])

        for side, j in enumerate(layers_of(d, width)):
            fresh = []
            for f in range(2):
                outer = 0.0
                for i in range(d + 1):
                    ghost = 4 + width + i if side else 3 - i
                    outer = outer + stencil_weights[4 - d + i] * field[slot, f, ghost, inner, :]
                fresh.append(field[1 - slot, f, 4 + j, inner, :] + courant[j] * (pending[f, j] + outer))
                final[f, j] = fresh[f]
            stacked[j, spot, :] = stacked[j, spot, :] + fresh[0] * fresh[1]

    def give(d):
        for b, (k, p) in enumerate(given):
            for i, j in enumerate(layers_of(d, width)):
                mate_out[d, b, i] = contribution(lax.rem(shot + k, n_shot), p, j)
        mate_copy(len(given), d).start()

    def gather(d):
        mate_copy(len(given), d).wait_recv()
        for b, (k, p) in enumerate(given):
            for i, j in enumerate(layers_of(d, width)):
                total = contribution(lax.rem(shot + k, n_shot), p, j) + mate_in[d, b, i]
                if k:
                    shot_out[k - 1, p, d, i] = total
                else:
                    image[j] = total
            if k:
                shot_copy(k, p, d).start()
        for i, j in enumerate(layers_of(d, width)):
            mate_out[d, 0, i] = contribution(shot, 1, j)
        mate_copy(1, d).start()

    def keep(d):
        mate_copy(1, d).wait_recv()
        for i, j in enumerate(layers_of(d, width)):
            image[j] = contribution(shot, 1, j) + mate_in[d, 0, i]

    source_copy = pltpu.make_async_copy(final.at[0], source_out.at[0], load_sem.at[0])
    recv_copy = pltpu.make_async_copy(final.at[1], recv_out.at[0], load_sem.at[1])
    image_copy = pltpu.make_async_copy(image, image_out, load_sem.at[2])

    @pl.when(pair == 0)
    def _():
        for d in range(4):
            finish(d)
            gather(d)
        image_copy.start()
        source_copy.start()
        recv_copy.start()
        arrived(mate_out.at[:, 0], mate_send.at[0])
        for k in range(1, n_shot):
            arrived(shot_out.at[k - 1], shot_send.at[k - 1])

    @pl.when(pair == 1)
    def _():
        for d in range(4):
            finish(d)
            give(d)
        source_copy.start()
        recv_copy.start()
        for d in range(4):
            keep(d)
        image_copy.start()
        arrived(mate_out, mate_send.at[0])

    @pl.when(both)
    def _():
        arrived(field.at[slot, :, 4:12, inner], last_send.at[0])

    @pl.when(single)
    def _():
        arrived(field.at[slot, :, 4:8, inner], last_send.at[0])

    for copy in (source_copy, recv_copy, image_copy):
        copy.wait()
    for k in range(1, n_shot):
        arrived(shot_in.at[k - 1], shot_recv.at[k - 1])


def deliver(own, incoming, source, recv, image_out, source_out, recv_out, image, sem):
    width = own.shape[0]
    copies = [
        pltpu.make_async_copy(source, source_out, sem.at[0]),
        pltpu.make_async_copy(recv, recv_out, sem.at[1]),
        pltpu.make_async_copy(image, image_out, sem.at[2]),
    ]
    copies[0].start()
    copies[1].start()
    for d in range(4):
        for i, j in enumerate(layers_of(d, width)):
            total = own[j]
            for k in range(incoming.shape[0]):
                total = total + incoming[k, d, i]
            image[j] = total
    copies[2].start()
    for copy in copies:
        copy.wait()


def solution(mesh):
    sizes = (mesh.shape["tile"], mesh.shape["shot"], mesh.shape["pair"])
    n_shot, n_pair = sizes[1:]

    def shards(velocity, anchors, source_prev, source_now, recv_prev, recv_now, source_x, source_yz, wavelet, recv_x, recv_yz, record):
        width, across, downward = source_now.shape[1:]
        owned = velocity.shape[1]
        survey = owned * n_shot * n_pair
        margin = survey - across
        f32 = jnp.float32
        piece = (4, 2, owned, downward)
        vmem = pl.BlockSpec(memory_space=pltpu.VMEM)
        anywhere = pl.BlockSpec(memory_space=pl.ANY)
        dma = pltpu.SemaphoreType.DMA
        record = jnp.swapaxes(record, 0, 1)
        shapes = (velocity.shape, source_now.shape, recv_now.shape)
        results = pl.pallas_call(
            functools.partial(kernel, sizes),
            out_shape=tuple(pltpu.VMEM(shape, f32) for shape in (shapes[0], (n_shot - 1,) + piece) + shapes[1:]),
            in_specs=[pl.BlockSpec(memory_space=pltpu.SMEM)] * 3 + [anywhere] * 9,
            out_specs=(anywhere,) * 4,
            scratch_shapes=[
                pltpu.SMEM(wavelet.shape, f32),
                pltpu.VMEM(recv_x.shape, jnp.int32),
                pltpu.VMEM(recv_yz.shape, jnp.int32),
                pltpu.VMEM(record.shape, f32),
                pltpu.VMEM((2, 2, width + 8, across + 2 * PAD, downward), f32),
                pltpu.VMEM((width, survey, downward), f32),
                pltpu.VMEM((width, across, downward), f32),
                pltpu.VMEM((width, across, downward), f32),
                pltpu.VMEM((2, width, across, downward), f32),
                pltpu.VMEM((width, across + 2 * margin, downward), f32),
                pltpu.VMEM((4, 2 * n_shot - 1) + piece[1:], f32),
                pltpu.VMEM((4, 2 * n_shot - 1) + piece[1:], f32),
                pltpu.VMEM((n_shot - 1, n_pair) + piece, f32),
                pltpu.VMEM(velocity.shape, f32),
                pltpu.VMEM((2, width, across, downward), f32),
                dma((4,)),
                dma((5,)),
                dma((2, 2)),
                dma((2, 2, CHUNKS)),
                dma((1,)),
                dma((4,)),
                dma((n_shot - 1, 2)),
                dma((n_shot - 1, 3)),
                dma((n_shot,)),
                dma((n_shot,)),
                dma((1,)),
                dma((4,)),
                dma((n_shot - 1,)),
                dma((n_shot - 1,)),
            ],
            compiler_params=pltpu.CompilerParams(
                collective_id=0, has_side_effects=True, vmem_limit_bytes=40 * 1024 * 1024
            ),
        )(*[
            pltpu.with_memory_space_constraint(operand, pltpu.HBM) if operand.size > 1 else operand
            for operand in (
                anchors, source_x, source_yz, wavelet, recv_x, recv_yz, record,
                velocity, source_prev, source_now, recv_prev, recv_now,
            )
        ])

        return pl.pallas_call(
            deliver,
            out_shape=[jax.ShapeDtypeStruct(shape, f32) for shape in shapes],
            in_specs=[vmem] * 4,
            out_specs=[anywhere] * 3,
            scratch_shapes=[pltpu.VMEM(velocity.shape, f32), dma((3,))],
        )(*[pltpu.with_memory_space_constraint(result, pltpu.VMEM) for result in results])

    in_specs = (
        P(("region", "tile"), ("shot", "pair"), None),
        P(("region", "shot")),
        P(("region", "shot", "pair"), "tile", None, None),
        P(("region", "shot", "pair"), "tile", None, None),
        P(("region", "shot", "pair"), "tile", None, None),
        P(("region", "shot", "pair"), "tile", None, None),
        P(("region", "shot", "pair")),
        P(("region", "shot", "pair")),
        P(("region", "shot", "pair"), None),
        P(("region", "shot", "pair"), None),
        P(("region", "shot", "pair"), None),
        P(("region", "shot", "pair"), None, None),
    )
    out_specs = (
        P(("region", "tile"), ("shot", "pair"), None),
        P(("region", "shot", "pair"), "tile", None, None),
        P(("region", "shot", "pair"), "tile", None, None),
    )
    return jax.shard_map(shards, mesh=mesh, in_specs=in_specs, out_specs=out_specs, check_vma=False)
```

```python
import functools

import jax
import jax.numpy as jnp
from jax import lax
from jax.experimental import pallas as pl
from jax.experimental.pallas import tpu as pltpu
from jax.sharding import PartitionSpec as P

STEPS = 6
MESH = pl.DeviceIdType.MESH

stencil_weights = (-205.0 / 72.0, 8.0 / 5.0, -1.0 / 5.0, 8.0 / 315.0, -1.0 / 560.0)
courant_scale = 0.1

PAD = 8
CHUNKS = 2
AHEAD = 3
SOON = 2
ORDER = ((1, 2), (0, 3), (1, 3))
REACH = 4


def layers_of(d, width):
    return (3 - d, width - 4 + d)


def kernel(
    sizes,
    anchors,
    source_x,
    source_yz,
    wavelet_in,
    recv_x_in,
    recv_yz_in,
    record_in,
    velocity,
    source_prev,
    source_now,
    recv_prev,
    recv_now,
    image_out,
    shot_in,
    source_out,
    recv_out,
    wavelet,
    recv_x,
    recv_yz,
    record,
    field,
    speed,
    courant,
    injected,
    pending,
    stacked,
    mate_out,
    mate_in,
    shot_out,
    image,
    final,
    small_sem,
    load_sem,
    halo_send,
    halo_recv,
    last_send,
    last_recv,
    speed_send,
    speed_recv,
    mate_speed_send,
    mate_speed_recv,
    mate_send,
    mate_recv,
    shot_send,
    shot_recv,
):
    n_tile, n_shot, n_pair = sizes
    width, across, downward = source_now.shape[1:]
    owned = velocity.shape[1]
    survey = owned * n_shot * n_pair
    margin = survey - across
    rows = across // CHUNKS
    tile = lax.axis_index("tile")
    shot = lax.axis_index("shot")
    pair = lax.axis_index("pair")
    mate = 1 - pair
    has_low = tile > 0
    has_high = tile < n_tile - 1
    has = (has_low, has_high)
    both = jnp.logical_and(has_low, has_high)
    single = jnp.logical_xor(has_low, has_high)

    def to_shot(k):
        return {"shot": lax.rem(shot + k, n_shot)}

    def to_shot_mate(k):
        return {"shot": lax.rem(shot + k, n_shot), "pair": mate}

    barrier = pltpu.get_barrier_semaphore()

    @pl.when(has_low)
    def _():
        pl.semaphore_signal(barrier, inc=1, device_id={"tile": tile - 1}, device_id_type=MESH)

    @pl.when(has_high)
    def _():
        pl.semaphore_signal(barrier, inc=1, device_id={"tile": tile + 1}, device_id_type=MESH)

    for k in range(1, n_shot):
        pl.semaphore_signal(barrier, inc=1, device_id=to_shot(k), device_id_type=MESH)
        pl.semaphore_signal(barrier, inc=1, device_id=to_shot_mate(k), device_id_type=MESH)
    pl.semaphore_signal(barrier, inc=1, device_id={"pair": mate}, device_id_type=MESH)

    def owner_rows(s, p):
        return pl.ds(pl.multiple_of((s * n_pair + p) * owned, owned), owned)

    inner = pl.ds(PAD, across)
    loads = [
        pltpu.make_async_copy(source_now.at[0], field.at[0, 0, 4 : 4 + width, inner], load_sem.at[0]),
        pltpu.make_async_copy(source_prev.at[0], field.at[1, 0, 4 : 4 + width, inner], load_sem.at[1]),
        pltpu.make_async_copy(recv_now.at[0], field.at[0, 1, 4 : 4 + width, inner], load_sem.at[2]),
        pltpu.make_async_copy(recv_prev.at[0], field.at[1, 1, 4 : 4 + width, inner], load_sem.at[1]),
        pltpu.make_async_copy(velocity, speed.at[:, owner_rows(shot, pair)], load_sem.at[3]),
    ]
    smalls = [
        pltpu.make_async_copy(source, target, small_sem.at[i])
        for i, (source, target) in enumerate(
            (
                (wavelet_in, wavelet),
                (recv_x_in, recv_x),
                (recv_yz_in, recv_yz),
                (record_in, record),
            )
        )
    ]
    for copy in loads + smalls:
        copy.start()

    for slot in range(2):
        for f in range(2):
            field[slot, f, 4 : 4 + width, 0:PAD] = jnp.zeros((width, PAD, downward), jnp.float32)
            field[slot, f, 4 : 4 + width, PAD + across : 2 * PAD + across] = jnp.zeros((width, PAD, downward), jnp.float32)

    def clear(first):
        def body(i, _):
            field[i // 8, (i // 4) % 2, first + i % 4] = jnp.zeros((across + 2 * PAD, downward), jnp.float32)
            return 0

        lax.fori_loop(0, 16, body, 0)

    @pl.when(jnp.logical_not(has_low))
    def _():
        clear(0)

    @pl.when(jnp.logical_not(has_high))
    def _():
        clear(4 + width)

    lane = lax.broadcasted_iota(jnp.int32, (1, 1, downward), 2)
    behind = [jnp.where(lane >= r, stencil_weights[r], 0.0) for r in range(1, 5)]
    ahead = [jnp.where(lane < downward - r, stencil_weights[r], 0.0) for r in range(1, 5)]
    shape = (width, 8, downward)
    local_cell = (
        lax.broadcasted_iota(jnp.int32, shape, 0) * (across * downward)
        + lax.broadcasted_iota(jnp.int32, shape, 1) * downward
        + lax.broadcasted_iota(jnp.int32, shape, 2)
    )
    for copy in smalls:
        copy.wait()
    first = tile * width
    source_cell = (source_x[0] - first) * (across * downward) + source_yz[0]

    place = (recv_x[...] - first) * across + recv_yz[...] // downward
    depth = recv_yz[...] % downward
    receivers = record.shape[2]
    cell = lax.broadcasted_iota(jnp.int32, (width * across, receivers), 0)
    pick = jnp.where(cell == place, 1.0, 0.0).astype(jnp.bfloat16)
    at_depth = lax.broadcasted_iota(jnp.int32, (downward, receivers), 0) == depth

    def clear_image(i, _):
        stacked[i] = jnp.zeros((2 * margin + across, downward), jnp.float32)
        return 0

    lax.fori_loop(0, width, clear_image, 0)

    neighbours = 2 * n_shot - 1 + has_low.astype(jnp.int32) + has_high.astype(jnp.int32)
    pl.semaphore_wait(barrier, neighbours)

    def halo(n, slot, f, c, side):
        landing = pl.ds(pl.multiple_of(PAD + c * rows, 8), rows)
        source, target, other = ((4, 4 + width, tile - 1), (width, 0, tile + 1))[side]
        return pltpu.make_async_remote_copy(
            field.at[slot, f, source : source + 4, landing],
            field.at[slot, f, target : target + 4, landing],
            halo_send.at[lax.rem(n, 2), f],
            halo_recv.at[lax.rem(n, 2), f, c],
            device_id={"tile": other},
            device_id_type=MESH,
        )

    last_slot = (STEPS - 1) % 2

    def last_halo(f, d, part, side):
        landing = inner if part is None else pl.ds(PAD + part * rows, rows)
        source, target, other = ((4 + d, 4 + width + d, tile - 1), (3 + width - d, 3 - d, tile + 1))[side]
        return pltpu.make_async_remote_copy(
            field.at[last_slot, f, source, landing],
            field.at[last_slot, f, target, landing],
            last_send.at[0],
            last_recv.at[d],
            device_id={"tile": other},
            device_id_type=MESH,
        )

    def last_halos(pieces):
        for side in range(2):
            @pl.when(has[side])
            def _():
                for f, d, part in pieces:
                    last_halo(f, d, part, side).start()

    def arrived(ref, sem):
        pltpu.make_async_copy(ref, ref, sem).wait()

    def first_halos(f):
        for c in range(CHUNKS):
            for side in range(2):
                @pl.when(has[side])
                def _():
                    halo(0, 0, f, c, side).start()

    forwarded = ((0, width // 2), (width // 2, width - 1))
    direct = (width - 1, width)

    def speed_copy(k, i):
        first, end = (forwarded + (direct, direct))[i]
        return pltpu.make_async_remote_copy(
            velocity.at[first:end],
            speed.at[first:end, owner_rows(shot, pair)],
            speed_send.at[k - 1, i // 2],
            speed_recv.at[k - 1, min(i, 2)],
            device_id=to_shot_mate(k) if i == 3 else to_shot(k),
            device_id_type=MESH,
        )

    for i in range(2):
        for k in range(1, n_shot):
            speed_copy(k, i).start()
    loads[0].wait()
    first_halos(0)
    pltpu.make_async_remote_copy(
        velocity,
        speed.at[:, owner_rows(shot, pair)],
        mate_speed_send.at[0],
        mate_speed_recv.at[0],
        device_id={"pair": mate},
        device_id_type=MESH,
    ).start()

    def inject(n):
        amount = record[n]
        high = amount.astype(jnp.bfloat16).astype(jnp.float32)
        rest = amount - high
        middle = rest.astype(jnp.bfloat16).astype(jnp.float32)
        low = rest - middle
        dense = jnp.zeros((width * across, downward), jnp.float32)
        for piece in (low, middle, high):
            spread = jnp.where(at_depth, piece, 0.0).astype(jnp.bfloat16)
            dense = dense + lax.dot_general(
                pick, spread, (((1,), (1,)), ((), ())), preferred_element_type=jnp.float32
            )
        injected[...] = dense.reshape(width, across, downward)

    def prepare(s, slot, f, y0, imaging):
        at = pl.multiple_of(PAD + y0, 8)
        centre = field[slot, f, 4 : 4 + width, pl.ds(at, 8), :]
        sums = (3.0 * stencil_weights[0]) * centre
        for r in range(1, 5):
            layers = []
            for j in range(width):
                layer = [centre[i : i + 1] for i in (j - r, j + r) if 0 <= i < width]
                layers.append(layer[0] if len(layer) == 1 else layer[0] + layer[1])
            near = jnp.concatenate(layers, axis=0)
            near = near + field[slot, f, 4 : 4 + width, pl.ds(at - r, 8), :]
            near = near + field[slot, f, 4 : 4 + width, pl.ds(at + r, 8), :]
            sums = sums + stencil_weights[r] * near
            sums = sums + behind[r - 1] * pltpu.roll(centre, r, 2)
            sums = sums + ahead[r - 1] * pltpu.roll(centre, downward - r, 2)
        older = field[1 - slot, f, 4 : 4 + width, pl.ds(at, 8), :]
        pending[f, :, pl.ds(y0, 8), :] = sums
        fresh = 2.0 * centre - older
        if f == 0:
            fresh = fresh + jnp.where(local_cell == source_cell - y0 * downward, wavelet[0, s], 0.0)
        else:
            fresh = fresh + injected[:, pl.ds(y0, 8), :]
        field[1 - slot, f, 4 : 4 + width, pl.ds(at, 8), :] = fresh
        if imaging:
            spot = pl.ds(pl.multiple_of(margin + y0, 8), 8)
            stacked[:, spot, :] = stacked[:, spot, :] + centre * field[slot, 0, 4 : 4 + width, pl.ds(at, 8), :]

    def prepare_all(s, f, imaging):
        if f == 1:
            inject(s)

        def ready(t, _):
            prepare(s, lax.rem(s, 2), f, pl.multiple_of(t * 8, 8), imaging)
            return 0

        lax.fori_loop(0, across // 8, ready, 0)

    def outer_low(low, j):
        term = stencil_weights[j + 1] * low[3:4]
        for r in range(j + 2, 5):
            term = term + stencil_weights[r] * low[4 + j - r : 5 + j - r]
        return term

    def outer_high(high, j):
        term = stencil_weights[4 - j] * high[0:1]
        for r in range(5 - j, 5):
            term = term + stencil_weights[r] * high[j - 4 + r : j - 3 + r]
        return term

    def complete(slot, f, y0):
        at = pl.multiple_of(PAD + y0, 8)
        gain = courant[:, pl.ds(y0, 8), :]
        low = field[slot, f, 0:4, pl.ds(at, 8), :]
        high = field[slot, f, 4 + width : 8 + width, pl.ds(at, 8), :]
        middle = [jnp.zeros((width - 8, 8, downward), jnp.float32)] if width > 8 else []
        outer = jnp.concatenate(
            [outer_low(low, j) for j in range(4)] + middle + [outer_high(high, j) for j in range(4)], axis=0
        )
        return field[1 - slot, f, 4 : 4 + width, pl.ds(at, 8), :] + gain * (pending[f, :, pl.ds(y0, 8), :] + outer)

    older = field.at[1, :, 4 : 4 + width, inner]
    arrived(older, load_sem.at[1])
    prepare_all(0, 0, False)
    loads[2].wait()
    prepare_all(0, 1, False)
    first_halos(1)
    for i in range(2, 4):
        for k in range(1, n_shot):
            speed_copy(k, i).start()

    def forward(k, i):
        piece_first, piece_end = forwarded[i]
        block = speed.at[piece_first:piece_end, owner_rows(lax.rem(shot + n_shot - k, n_shot), pair)]
        return pltpu.make_async_remote_copy(
            block,
            block,
            mate_speed_send.at[k],
            mate_speed_recv.at[k],
            device_id={"pair": mate},
            device_id_type=MESH,
        )

    for i in range(2):
        for k in range(1, n_shot):
            speed_copy(k, i).wait_recv()
            forward(k, i).start()


    loads[4].wait()
    pltpu.make_async_remote_copy(
        velocity,
        speed.at[:, owner_rows(shot, mate)],
        mate_speed_send.at[0],
        mate_speed_recv.at[0],
        device_id={"pair": mate},
        device_id_type=MESH,
    ).wait()
    sent = velocity.at[: forwarded[1][1]]
    twice = velocity.at[: 2 * (direct[1] - direct[0])]
    for k in range(1, n_shot):
        arrived(sent, mate_speed_recv.at[k])
        arrived(twice, speed_recv.at[k - 1, 2])
        arrived(sent, speed_send.at[k - 1, 0])
        arrived(twice, speed_send.at[k - 1, 1])
        arrived(sent, mate_speed_send.at[k])

    start_row = anchors[0]

    def refresh(i, _):
        scaled = speed[i, pl.ds(start_row, across), :] * courant_scale
        courant[i] = scaled * scaled
        return 0

    lax.fori_loop(0, width, refresh, 0)

    def settle(s, f):
        @pl.when(both)
        def _():
            arrived(field.at[0, f, 4:12, inner], halo_send.at[lax.rem(s, 2), f])

        @pl.when(single)
        def _():
            arrived(field.at[0, f, 4:8, inner], halo_send.at[lax.rem(s, 2), f])

    def await_halo(s, slot, f, c):
        landing = pl.ds(PAD + c * rows, rows)

        @pl.when(both)
        def _():
            arrived(field.at[slot, f, 4:12, landing], halo_recv.at[lax.rem(s, 2), f, c])

        @pl.when(single)
        def _():
            arrived(field.at[slot, f, 4:8, landing], halo_recv.at[lax.rem(s, 2), f, c])

    def step(s, _):
        slot = lax.rem(s, 2)
        for f in range(2):
            for c in range(CHUNKS):
                await_halo(s, slot, f, c)

                def tiles(t, _):
                    y0 = pl.multiple_of(c * rows + t * 8, 8)
                    field[1 - slot, f, 4 : 4 + width, pl.ds(pl.multiple_of(PAD + y0, 8), 8), :] = complete(slot, f, y0)
                    return 0

                lax.fori_loop(0, rows // 8, tiles, 0)
                for side in range(2):
                    @pl.when(jnp.logical_and(has[side], s < STEPS - 2))
                    def _():
                        halo(s + 1, 1 - slot, f, c, side).start()

                if f == 1:
                    @pl.when(s == STEPS - 2)
                    def _():
                        last_halos([(1, d, c) for d in range(SOON)])
                        if c == CHUNKS - 1:
                            last_halos([(e, d, None) for e, d in ORDER])

            if f == 0:
                @pl.when(s == STEPS - 2)
                def _():
                    last_halos([(0, d, None) for d in range(AHEAD)])

            settle(s, f)
            prepare_all(s + 1, f, f == 1)

        return 0

    lax.fori_loop(0, STEPS - 1, step, 0)

    slot = last_slot
    spot = pl.ds(margin, across)

    def contribution(s, p, j):
        return stacked[j, pl.ds((s * n_pair + p) * owned + margin - start_row, owned), :]

    def mate_copy(blocks, d):
        return pltpu.make_async_remote_copy(
            mate_out.at[d, :blocks],
            mate_in.at[d, :blocks],
            mate_send.at[0],
            mate_recv.at[d],
            device_id={"pair": mate},
            device_id_type=MESH,
        )

    def shot_copy(k, p, d):
        return pltpu.make_async_remote_copy(
            shot_out.at[k - 1, p, d],
            shot_in.at[k - 1, d],
            shot_send.at[k - 1],
            shot_recv.at[k - 1],
            device_id={"shot": lax.rem(shot + k, n_shot), "pair": p},
            device_id_type=MESH,
        )

    given = [(k, p) for k in range(1, n_shot) for p in range(n_pair)] + [(0, 0)]

    def finish(d):
        @pl.when(both)
        def _():
            arrived(field.at[slot, :, 4:6, inner], last_recv.at[d])

        @pl.when(single)
        def _():
            arrived(field.at[slot, :, 4:5, inner], last_recv.at[d])

        for side, j in enumerate(layers_of(d, width)):
            fresh = []
            for f in range(2):
                outer = 0.0
                for i in range(d + 1):
                    ghost = 4 + width + i if side else 3 - i
                    outer = outer + stencil_weights[4 - d + i] * field[slot, f, ghost, inner, :]
                fresh.append(field[1 - slot, f, 4 + j, inner, :] + courant[j] * (pending[f, j] + outer))
                final[f, j] = fresh[f]
            stacked[j, spot, :] = stacked[j, spot, :] + fresh[0] * fresh[1]

    def give(d):
        for b, (k, p) in enumerate(given):
            for i, j in enumerate(layers_of(d, width)):
                mate_out[d, b, i] = contribution(lax.rem(shot + k, n_shot), p, j)
        mate_copy(len(given), d).start()

    def gather(d):
        mate_copy(len(given), d).wait_recv()
        for b, (k, p) in enumerate(given):
            for i, j in enumerate(layers_of(d, width)):
                total = contribution(lax.rem(shot + k, n_shot), p, j) + mate_in[d, b, i]
                if k:
                    shot_out[k - 1, p, d, i] = total
                else:
                    image[j] = total
            if k:
                shot_copy(k, p, d).start()
        for i, j in enumerate(layers_of(d, width)):
            mate_out[d, 0, i] = contribution(shot, 1, j)
        mate_copy(1, d).start()

    def keep(d):
        mate_copy(1, d).wait_recv()
        for i, j in enumerate(layers_of(d, width)):
            image[j] = contribution(shot, 1, j) + mate_in[d, 0, i]

    source_copy = pltpu.make_async_copy(final.at[0], source_out.at[0], load_sem.at[0])
    recv_copy = pltpu.make_async_copy(final.at[1], recv_out.at[0], load_sem.at[1])
    image_copy = pltpu.make_async_copy(image, image_out, load_sem.at[2])

    @pl.when(pair == 0)
    def _():
        for d in range(4):
            finish(d)
            gather(d)
        image_copy.start()
        source_copy.start()
        recv_copy.start()
        arrived(mate_out.at[:, 0], mate_send.at[0])
        for k in range(1, n_shot):
            arrived(shot_out.at[k - 1], shot_send.at[k - 1])

    @pl.when(pair == 1)
    def _():
        for d in range(4):
            finish(d)
            give(d)
        source_copy.start()
        recv_copy.start()
        for d in range(4):
            keep(d)
        image_copy.start()
        arrived(mate_out, mate_send.at[0])

    @pl.when(both)
    def _():
        arrived(field.at[slot, :, 4:12, inner], last_send.at[0])

    @pl.when(single)
    def _():
        arrived(field.at[slot, :, 4:8, inner], last_send.at[0])

    for copy in (source_copy, recv_copy, image_copy):
        copy.wait()
    for k in range(1, n_shot):
        arrived(shot_in.at[k - 1], shot_recv.at[k - 1])


def deliver(own, incoming, source, recv, image_out, source_out, recv_out, image, sem):
    width = own.shape[0]
    copies = [
        pltpu.make_async_copy(source, source_out, sem.at[0]),
        pltpu.make_async_copy(recv, recv_out, sem.at[1]),
        pltpu.make_async_copy(image, image_out, sem.at[2]),
    ]
    copies[0].start()
    copies[1].start()
    for d in range(4):
        for i, j in enumerate(layers_of(d, width)):
            total = own[j]
            for k in range(incoming.shape[0]):
                total = total + incoming[k, d, i]
            image[j] = total
    copies[2].start()
    for copy in copies:
        copy.wait()


def solution(mesh):
    sizes = (mesh.shape["tile"], mesh.shape["shot"], mesh.shape["pair"])
    n_shot, n_pair = sizes[1:]

    def shards(velocity, anchors, source_prev, source_now, recv_prev, recv_now, source_x, source_yz, wavelet, recv_x, recv_yz, record):
        width, across, downward = source_now.shape[1:]
        owned = velocity.shape[1]
        survey = owned * n_shot * n_pair
        margin = survey - across
        f32 = jnp.float32
        piece = (4, 2, owned, downward)
        vmem = pl.BlockSpec(memory_space=pltpu.VMEM)
        anywhere = pl.BlockSpec(memory_space=pl.ANY)
        dma = pltpu.SemaphoreType.DMA
        record = jnp.swapaxes(record, 0, 1)
        shapes = (velocity.shape, source_now.shape, recv_now.shape)
        results = pl.pallas_call(
            functools.partial(kernel, sizes),
            out_shape=tuple(pltpu.VMEM(shape, f32) for shape in (shapes[0], (n_shot - 1,) + piece) + shapes[1:]),
            in_specs=[pl.BlockSpec(memory_space=pltpu.SMEM)] * 3 + [anywhere] * 9,
            out_specs=(anywhere,) * 4,
            scratch_shapes=[
                pltpu.SMEM(wavelet.shape, f32),
                pltpu.VMEM(recv_x.shape, jnp.int32),
                pltpu.VMEM(recv_yz.shape, jnp.int32),
                pltpu.VMEM(record.shape, f32),
                pltpu.VMEM((2, 2, width + 8, across + 2 * PAD, downward), f32),
                pltpu.VMEM((width, survey, downward), f32),
                pltpu.VMEM((width, across, downward), f32),
                pltpu.VMEM((width, across, downward), f32),
                pltpu.VMEM((2, width, across, downward), f32),
                pltpu.VMEM((width, across + 2 * margin, downward), f32),
                pltpu.VMEM((4, 2 * n_shot - 1) + piece[1:], f32),
                pltpu.VMEM((4, 2 * n_shot - 1) + piece[1:], f32),
                pltpu.VMEM((n_shot - 1, n_pair) + piece, f32),
                pltpu.VMEM(velocity.shape, f32),
                pltpu.VMEM((2, width, across, downward), f32),
                dma((4,)),
                dma((4,)),
                dma((2, 2)),
                dma((2, 2, CHUNKS)),
                dma((1,)),
                dma((4,)),
                dma((n_shot - 1, 2)),
                dma((n_shot - 1, 3)),
                dma((n_shot,)),
                dma((n_shot,)),
                dma((1,)),
                dma((4,)),
                dma((n_shot - 1,)),
                dma((n_shot - 1,)),
            ],
            compiler_params=pltpu.CompilerParams(
                collective_id=0, has_side_effects=True, vmem_limit_bytes=40 * 1024 * 1024
            ),
        )(*[
            pltpu.with_memory_space_constraint(operand, pltpu.HBM) if operand.size > 1 else operand
            for operand in (
                anchors, source_x, source_yz, wavelet, recv_x, recv_yz, record,
                velocity, source_prev, source_now, recv_prev, recv_now,
            )
        ])

        return pl.pallas_call(
            deliver,
            out_shape=[jax.ShapeDtypeStruct(shape, f32) for shape in shapes],
            in_specs=[vmem] * 4,
            out_specs=[anywhere] * 3,
            scratch_shapes=[pltpu.VMEM(velocity.shape, f32), dma((3,))],
        )(*[pltpu.with_memory_space_constraint(result, pltpu.VMEM) for result in results])

    in_specs = (
        P(("region", "tile"), ("shot", "pair"), None),
        P(("region", "shot")),
        P(("region", "shot", "pair"), "tile", None, None),
        P(("region", "shot", "pair"), "tile", None, None),
        P(("region", "shot", "pair"), "tile", None, None),
        P(("region", "shot", "pair"), "tile", None, None),
        P(("region", "shot", "pair")),
        P(("region", "shot", "pair")),
        P(("region", "shot", "pair"), None),
        P(("region", "shot", "pair"), None),
        P(("region", "shot", "pair"), None),
        P(("region", "shot", "pair"), None, None),
    )
    out_specs = (
        P(("region", "tile"), ("shot", "pair"), None),
        P(("region", "shot", "pair"), "tile", None, None),
        P(("region", "shot", "pair"), "tile", None, None),
    )
    return jax.shard_map(shards, mesh=mesh, in_specs=in_specs, out_specs=out_specs, check_vma=False)
```

```python
import functools

import jax
import jax.numpy as jnp
from jax import lax
from jax.experimental import pallas as pl
from jax.experimental.pallas import tpu as pltpu
from jax.sharding import PartitionSpec as P

STEPS = 6
MESH = pl.DeviceIdType.MESH

stencil_weights = (-205.0 / 72.0, 8.0 / 5.0, -1.0 / 5.0, 8.0 / 315.0, -1.0 / 560.0)
courant_scale = 0.1

PAD = 8
CHUNKS = 2
AHEAD = 3
SOON = 2
ORDER = ((0, 3), (1, 2), (1, 3))
REACH = 4


def layers_of(d, width):
    return (3 - d, width - 4 + d)


def kernel(
    sizes,
    anchors,
    source_x,
    source_yz,
    wavelet_in,
    recv_x_in,
    recv_yz_in,
    record_in,
    velocity,
    source_prev,
    source_now,
    recv_prev,
    recv_now,
    image_out,
    shot_in,
    source_out,
    recv_out,
    wavelet,
    recv_x,
    recv_yz,
    record,
    field,
    speed,
    courant,
    injected,
    pending,
    stacked,
    mate_out,
    mate_in,
    shot_out,
    image,
    final,
    small_sem,
    load_sem,
    halo_send,
    halo_recv,
    last_send,
    last_recv,
    speed_send,
    speed_recv,
    mate_speed_send,
    mate_speed_recv,
    mate_send,
    mate_recv,
    shot_send,
    shot_recv,
):
    n_tile, n_shot, n_pair = sizes
    width, across, downward = source_now.shape[1:]
    owned = velocity.shape[1]
    survey = owned * n_shot * n_pair
    margin = survey - across
    rows = across // CHUNKS
    tile = lax.axis_index("tile")
    shot = lax.axis_index("shot")
    pair = lax.axis_index("pair")
    mate = 1 - pair
    has_low = tile > 0
    has_high = tile < n_tile - 1
    has = (has_low, has_high)
    both = jnp.logical_and(has_low, has_high)
    single = jnp.logical_xor(has_low, has_high)

    def to_shot(k):
        return {"shot": lax.rem(shot + k, n_shot)}

    def to_shot_mate(k):
        return {"shot": lax.rem(shot + k, n_shot), "pair": mate}

    barrier = pltpu.get_barrier_semaphore()

    @pl.when(has_low)
    def _():
        pl.semaphore_signal(barrier, inc=1, device_id={"tile": tile - 1}, device_id_type=MESH)

    @pl.when(has_high)
    def _():
        pl.semaphore_signal(barrier, inc=1, device_id={"tile": tile + 1}, device_id_type=MESH)

    for k in range(1, n_shot):
        pl.semaphore_signal(barrier, inc=1, device_id=to_shot(k), device_id_type=MESH)
        pl.semaphore_signal(barrier, inc=1, device_id=to_shot_mate(k), device_id_type=MESH)
    pl.semaphore_signal(barrier, inc=1, device_id={"pair": mate}, device_id_type=MESH)

    def owner_rows(s, p):
        return pl.ds(pl.multiple_of((s * n_pair + p) * owned, owned), owned)

    inner = pl.ds(PAD, across)
    loads = [
        pltpu.make_async_copy(source_now.at[0], field.at[0, 0, 4 : 4 + width, inner], load_sem.at[0]),
        pltpu.make_async_copy(source_prev.at[0], field.at[1, 0, 4 : 4 + width, inner], load_sem.at[1]),
        pltpu.make_async_copy(recv_now.at[0], field.at[0, 1, 4 : 4 + width, inner], load_sem.at[2]),
        pltpu.make_async_copy(recv_prev.at[0], field.at[1, 1, 4 : 4 + width, inner], load_sem.at[1]),
        pltpu.make_async_copy(velocity, speed.at[:, owner_rows(shot, pair)], load_sem.at[3]),
    ]
    smalls = [
        pltpu.make_async_copy(source, target, small_sem.at[i])
        for i, (source, target) in enumerate(
            (
                (wavelet_in, wavelet),
                (recv_x_in, recv_x),
                (recv_yz_in, recv_yz),
                (record_in, record),
            )
        )
    ]
    for copy in loads + smalls:
        copy.start()

    for slot in range(2):
        for f in range(2):
            field[slot, f, 4 : 4 + width, 0:PAD] = jnp.zeros((width, PAD, downward), jnp.float32)
            field[slot, f, 4 : 4 + width, PAD + across : 2 * PAD + across] = jnp.zeros((width, PAD, downward), jnp.float32)

    def clear(first):
        def body(i, _):
            field[i // 8, (i // 4) % 2, first + i % 4] = jnp.zeros((across + 2 * PAD, downward), jnp.float32)
            return 0

        lax.fori_loop(0, 16, body, 0)

    @pl.when(jnp.logical_not(has_low))
    def _():
        clear(0)

    @pl.when(jnp.logical_not(has_high))
    def _():
        clear(4 + width)

    lane = lax.broadcasted_iota(jnp.int32, (1, 1, downward), 2)
    behind = [jnp.where(lane >= r, stencil_weights[r], 0.0) for r in range(1, 5)]
    ahead = [jnp.where(lane < downward - r, stencil_weights[r], 0.0) for r in range(1, 5)]
    shape = (width, 8, downward)
    local_cell = (
        lax.broadcasted_iota(jnp.int32, shape, 0) * (across * downward)
        + lax.broadcasted_iota(jnp.int32, shape, 1) * downward
        + lax.broadcasted_iota(jnp.int32, shape, 2)
    )
    for copy in smalls:
        copy.wait()
    first = tile * width
    source_cell = (source_x[0] - first) * (across * downward) + source_yz[0]

    place = (recv_x[...] - first) * across + recv_yz[...] // downward
    depth = recv_yz[...] % downward
    receivers = record.shape[2]
    cell = lax.broadcasted_iota(jnp.int32, (width * across, receivers), 0)
    pick = jnp.where(cell == place, 1.0, 0.0).astype(jnp.bfloat16)
    at_depth = lax.broadcasted_iota(jnp.int32, (downward, receivers), 0) == depth

    def clear_image(i, _):
        stacked[i] = jnp.zeros((2 * margin + across, downward), jnp.float32)
        return 0

    lax.fori_loop(0, width, clear_image, 0)

    neighbours = 2 * n_shot - 1 + has_low.astype(jnp.int32) + has_high.astype(jnp.int32)
    pl.semaphore_wait(barrier, neighbours)

    def halo(n, slot, f, c, side):
        landing = pl.ds(pl.multiple_of(PAD + c * rows, 8), rows)
        source, target, other = ((4, 4 + width, tile - 1), (width, 0, tile + 1))[side]
        return pltpu.make_async_remote_copy(
            field.at[slot, f, source : source + 4, landing],
            field.at[slot, f, target : target + 4, landing],
            halo_send.at[lax.rem(n, 2), f],
            halo_recv.at[lax.rem(n, 2), f, c],
            device_id={"tile": other},
            device_id_type=MESH,
        )

    last_slot = (STEPS - 1) % 2

    def last_halo(f, d, part, side):
        landing = inner if part is None else pl.ds(PAD + part * rows, rows)
        source, target, other = ((4 + d, 4 + width + d, tile - 1), (3 + width - d, 3 - d, tile + 1))[side]
        return pltpu.make_async_remote_copy(
            field.at[last_slot, f, source, landing],
            field.at[last_slot, f, target, landing],
            last_send.at[0],
            last_recv.at[d],
            device_id={"tile": other},
            device_id_type=MESH,
        )

    def last_halos(pieces):
        for side in range(2):
            @pl.when(has[side])
            def _():
                for f, d, part in pieces:
                    last_halo(f, d, part, side).start()

    def arrived(ref, sem):
        pltpu.make_async_copy(ref, ref, sem).wait()

    def first_halos(f):
        for c in range(CHUNKS):
            for side in range(2):
                @pl.when(has[side])
                def _():
                    halo(0, 0, f, c, side).start()

    forwarded = ((0, width // 2), (width // 2, width - 1))
    direct = (width - 1, width)

    def speed_copy(k, i):
        first, end = (forwarded + (direct, direct))[i]
        return pltpu.make_async_remote_copy(
            velocity.at[first:end],
            speed.at[first:end, owner_rows(shot, pair)],
            speed_send.at[k - 1, i // 2],
            speed_recv.at[k - 1, min(i, 2)],
            device_id=to_shot_mate(k) if i == 3 else to_shot(k),
            device_id_type=MESH,
        )

    for i in range(2):
        for k in range(1, n_shot):
            speed_copy(k, i).start()
    loads[0].wait()
    first_halos(0)
    pltpu.make_async_remote_copy(
        velocity,
        speed.at[:, owner_rows(shot, pair)],
        mate_speed_send.at[0],
        mate_speed_recv.at[0],
        device_id={"pair": mate},
        device_id_type=MESH,
    ).start()

    def inject(n):
        amount = record[n]
        high = amount.astype(jnp.bfloat16).astype(jnp.float32)
        rest = amount - high
        middle = rest.astype(jnp.bfloat16).astype(jnp.float32)
        low = rest - middle
        dense = jnp.zeros((width * across, downward), jnp.float32)
        for piece in (low, middle, high):
            spread = jnp.where(at_depth, piece, 0.0).astype(jnp.bfloat16)
            dense = dense + lax.dot_general(
                pick, spread, (((1,), (1,)), ((), ())), preferred_element_type=jnp.float32
            )
        injected[...] = dense.reshape(width, across, downward)

    def prepare(s, slot, f, y0, imaging):
        at = pl.multiple_of(PAD + y0, 8)
        centre = field[slot, f, 4 : 4 + width, pl.ds(at, 8), :]
        sums = (3.0 * stencil_weights[0]) * centre
        for r in range(1, 5):
            layers = []
            for j in range(width):
                layer = [centre[i : i + 1] for i in (j - r, j + r) if 0 <= i < width]
                layers.append(layer[0] if len(layer) == 1 else layer[0] + layer[1])
            near = jnp.concatenate(layers, axis=0)
            near = near + field[slot, f, 4 : 4 + width, pl.ds(at - r, 8), :]
            near = near + field[slot, f, 4 : 4 + width, pl.ds(at + r, 8), :]
            sums = sums + stencil_weights[r] * near
            sums = sums + behind[r - 1] * pltpu.roll(centre, r, 2)
            sums = sums + ahead[r - 1] * pltpu.roll(centre, downward - r, 2)
        older = field[1 - slot, f, 4 : 4 + width, pl.ds(at, 8), :]
        pending[f, :, pl.ds(y0, 8), :] = sums
        fresh = 2.0 * centre - older
        if f == 0:
            fresh = fresh + jnp.where(local_cell == source_cell - y0 * downward, wavelet[0, s], 0.0)
        else:
            fresh = fresh + injected[:, pl.ds(y0, 8), :]
        field[1 - slot, f, 4 : 4 + width, pl.ds(at, 8), :] = fresh
        if imaging:
            spot = pl.ds(pl.multiple_of(margin + y0, 8), 8)
            stacked[:, spot, :] = stacked[:, spot, :] + centre * field[slot, 0, 4 : 4 + width, pl.ds(at, 8), :]

    def prepare_all(s, f, imaging):
        if f == 1:
            inject(s)

        def ready(t, _):
            prepare(s, lax.rem(s, 2), f, pl.multiple_of(t * 8, 8), imaging)
            return 0

        lax.fori_loop(0, across // 8, ready, 0)

    def outer_low(low, j):
        term = stencil_weights[j + 1] * low[3:4]
        for r in range(j + 2, 5):
            term = term + stencil_weights[r] * low[4 + j - r : 5 + j - r]
        return term

    def outer_high(high, j):
        term = stencil_weights[4 - j] * high[0:1]
        for r in range(5 - j, 5):
            term = term + stencil_weights[r] * high[j - 4 + r : j - 3 + r]
        return term

    def complete(slot, f, y0):
        at = pl.multiple_of(PAD + y0, 8)
        gain = courant[:, pl.ds(y0, 8), :]
        low = field[slot, f, 0:4, pl.ds(at, 8), :]
        high = field[slot, f, 4 + width : 8 + width, pl.ds(at, 8), :]
        middle = [jnp.zeros((width - 8, 8, downward), jnp.float32)] if width > 8 else []
        outer = jnp.concatenate(
            [outer_low(low, j) for j in range(4)] + middle + [outer_high(high, j) for j in range(4)], axis=0
        )
        return field[1 - slot, f, 4 : 4 + width, pl.ds(at, 8), :] + gain * (pending[f, :, pl.ds(y0, 8), :] + outer)

    older = field.at[1, :, 4 : 4 + width, inner]
    arrived(older, load_sem.at[1])
    prepare_all(0, 0, False)
    loads[2].wait()
    prepare_all(0, 1, False)
    first_halos(1)
    for i in range(2, 4):
        for k in range(1, n_shot):
            speed_copy(k, i).start()

    def forward(k, i):
        piece_first, piece_end = forwarded[i]
        block = speed.at[piece_first:piece_end, owner_rows(lax.rem(shot + n_shot - k, n_shot), pair)]
        return pltpu.make_async_remote_copy(
            block,
            block,
            mate_speed_send.at[k],
            mate_speed_recv.at[k],
            device_id={"pair": mate},
            device_id_type=MESH,
        )

    for i in range(2):
        for k in range(1, n_shot):
            speed_copy(k, i).wait_recv()
            forward(k, i).start()


    loads[4].wait()
    pltpu.make_async_remote_copy(
        velocity,
        speed.at[:, owner_rows(shot, mate)],
        mate_speed_send.at[0],
        mate_speed_recv.at[0],
        device_id={"pair": mate},
        device_id_type=MESH,
    ).wait()
    sent = velocity.at[: forwarded[1][1]]
    twice = velocity.at[: 2 * (direct[1] - direct[0])]
    for k in range(1, n_shot):
        arrived(sent, mate_speed_recv.at[k])
        arrived(twice, speed_recv.at[k - 1, 2])
        arrived(sent, speed_send.at[k - 1, 0])
        arrived(twice, speed_send.at[k - 1, 1])
        arrived(sent, mate_speed_send.at[k])

    start_row = anchors[0]

    def refresh(i, _):
        scaled = speed[i, pl.ds(start_row, across), :] * courant_scale
        courant[i] = scaled * scaled
        return 0

    lax.fori_loop(0, width, refresh, 0)

    def settle(s, f):
        @pl.when(both)
        def _():
            arrived(field.at[0, f, 4:12, inner], halo_send.at[lax.rem(s, 2), f])

        @pl.when(single)
        def _():
            arrived(field.at[0, f, 4:8, inner], halo_send.at[lax.rem(s, 2), f])

    def await_halo(s, slot, f, c):
        landing = pl.ds(PAD + c * rows, rows)

        @pl.when(both)
        def _():
            arrived(field.at[slot, f, 4:12, landing], halo_recv.at[lax.rem(s, 2), f, c])

        @pl.when(single)
        def _():
            arrived(field.at[slot, f, 4:8, landing], halo_recv.at[lax.rem(s, 2), f, c])

    def step(s, _):
        slot = lax.rem(s, 2)
        for f in range(2):
            for c in range(CHUNKS):
                await_halo(s, slot, f, c)

                def tiles(t, _):
                    y0 = pl.multiple_of(c * rows + t * 8, 8)
                    field[1 - slot, f, 4 : 4 + width, pl.ds(pl.multiple_of(PAD + y0, 8), 8), :] = complete(slot, f, y0)
                    return 0

                lax.fori_loop(0, rows // 8, tiles, 0)
                for side in range(2):
                    @pl.when(jnp.logical_and(has[side], s < STEPS - 2))
                    def _():
                        halo(s + 1, 1 - slot, f, c, side).start()

                if f == 1:
                    @pl.when(s == STEPS - 2)
                    def _():
                        last_halos([(1, d, c) for d in range(SOON)])
                        if c == CHUNKS - 1:
                            last_halos([(e, d, None) for e, d in ORDER])

            if f == 0:
                @pl.when(s == STEPS - 2)
                def _():
                    last_halos([(0, d, None) for d in range(AHEAD)])

            settle(s, f)
            prepare_all(s + 1, f, f == 1)

        return 0

    lax.fori_loop(0, STEPS - 1, step, 0)

    slot = last_slot
    spot = pl.ds(margin, across)

    def contribution(s, p, j):
        return stacked[j, pl.ds((s * n_pair + p) * owned + margin - start_row, owned), :]

    def mate_copy(blocks, d):
        return pltpu.make_async_remote_copy(
            mate_out.at[d, :blocks],
            mate_in.at[d, :blocks],
            mate_send.at[0],
            mate_recv.at[d],
            device_id={"pair": mate},
            device_id_type=MESH,
        )

    def shot_copy(k, p, d):
        return pltpu.make_async_remote_copy(
            shot_out.at[k - 1, p, d],
            shot_in.at[k - 1, d],
            shot_send.at[k - 1],
            shot_recv.at[k - 1],
            device_id={"shot": lax.rem(shot + k, n_shot), "pair": p},
            device_id_type=MESH,
        )

    given = [(k, p) for k in range(1, n_shot) for p in range(n_pair)] + [(0, 0)]

    def finish(d):
        @pl.when(both)
        def _():
            arrived(field.at[slot, :, 4:6, inner], last_recv.at[d])

        @pl.when(single)
        def _():
            arrived(field.at[slot, :, 4:5, inner], last_recv.at[d])

        for side, j in enumerate(layers_of(d, width)):
            fresh = []
            for f in range(2):
                outer = 0.0
                for i in range(d + 1):
                    ghost = 4 + width + i if side else 3 - i
                    outer = outer + stencil_weights[4 - d + i] * field[slot, f, ghost, inner, :]
                fresh.append(field[1 - slot, f, 4 + j, inner, :] + courant[j] * (pending[f, j] + outer))
                final[f, j] = fresh[f]
            stacked[j, spot, :] = stacked[j, spot, :] + fresh[0] * fresh[1]

    def give(d):
        for b, (k, p) in enumerate(given):
            for i, j in enumerate(layers_of(d, width)):
                mate_out[d, b, i] = contribution(lax.rem(shot + k, n_shot), p, j)
        mate_copy(len(given), d).start()

    def gather(d):
        mate_copy(len(given), d).wait_recv()
        for b, (k, p) in enumerate(given):
            for i, j in enumerate(layers_of(d, width)):
                total = contribution(lax.rem(shot + k, n_shot), p, j) + mate_in[d, b, i]
                if k:
                    shot_out[k - 1, p, d, i] = total
                else:
                    image[j] = total
            if k:
                shot_copy(k, p, d).start()
        for i, j in enumerate(layers_of(d, width)):
            mate_out[d, 0, i] = contribution(shot, 1, j)
        mate_copy(1, d).start()

    def keep(d):
        mate_copy(1, d).wait_recv()
        for i, j in enumerate(layers_of(d, width)):
            image[j] = contribution(shot, 1, j) + mate_in[d, 0, i]

    source_copy = pltpu.make_async_copy(final.at[0], source_out.at[0], load_sem.at[0])
    recv_copy = pltpu.make_async_copy(final.at[1], recv_out.at[0], load_sem.at[1])
    image_copy = pltpu.make_async_copy(image, image_out, load_sem.at[2])

    @pl.when(pair == 0)
    def _():
        for d in range(4):
            finish(d)
            gather(d)
        image_copy.start()
        source_copy.start()
        recv_copy.start()
        arrived(mate_out.at[:, 0], mate_send.at[0])
        for k in range(1, n_shot):
            arrived(shot_out.at[k - 1], shot_send.at[k - 1])

    @pl.when(pair == 1)
    def _():
        for d in range(4):
            finish(d)
            give(d)
        source_copy.start()
        recv_copy.start()
        for d in range(4):
            keep(d)
        image_copy.start()
        arrived(mate_out, mate_send.at[0])

    @pl.when(both)
    def _():
        arrived(field.at[slot, :, 4:12, inner], last_send.at[0])

    @pl.when(single)
    def _():
        arrived(field.at[slot, :, 4:8, inner], last_send.at[0])

    for copy in (source_copy, recv_copy, image_copy):
        copy.wait()
    for k in range(1, n_shot):
        arrived(shot_in.at[k - 1], shot_recv.at[k - 1])


def deliver(own, incoming, source, recv, image_out, source_out, recv_out, image, sem):
    width = own.shape[0]
    copies = [
        pltpu.make_async_copy(source, source_out, sem.at[0]),
        pltpu.make_async_copy(recv, recv_out, sem.at[1]),
        pltpu.make_async_copy(image, image_out, sem.at[2]),
    ]
    copies[0].start()
    copies[1].start()
    for d in range(4):
        for i, j in enumerate(layers_of(d, width)):
            total = own[j]
            for k in range(incoming.shape[0]):
                total = total + incoming[k, d, i]
            image[j] = total
    copies[2].start()
    for copy in copies:
        copy.wait()


def solution(mesh):
    sizes = (mesh.shape["tile"], mesh.shape["shot"], mesh.shape["pair"])
    n_shot, n_pair = sizes[1:]

    def shards(velocity, anchors, source_prev, source_now, recv_prev, recv_now, source_x, source_yz, wavelet, recv_x, recv_yz, record):
        width, across, downward = source_now.shape[1:]
        owned = velocity.shape[1]
        survey = owned * n_shot * n_pair
        margin = survey - across
        f32 = jnp.float32
        piece = (4, 2, owned, downward)
        vmem = pl.BlockSpec(memory_space=pltpu.VMEM)
        anywhere = pl.BlockSpec(memory_space=pl.ANY)
        dma = pltpu.SemaphoreType.DMA
        record = jnp.swapaxes(record, 0, 1)
        shapes = (velocity.shape, source_now.shape, recv_now.shape)
        results = pl.pallas_call(
            functools.partial(kernel, sizes),
            out_shape=tuple(pltpu.VMEM(shape, f32) for shape in (shapes[0], (n_shot - 1,) + piece) + shapes[1:]),
            in_specs=[pl.BlockSpec(memory_space=pltpu.SMEM)] * 3 + [anywhere] * 9,
            out_specs=(anywhere,) * 4,
            scratch_shapes=[
                pltpu.SMEM(wavelet.shape, f32),
                pltpu.VMEM(recv_x.shape, jnp.int32),
                pltpu.VMEM(recv_yz.shape, jnp.int32),
                pltpu.VMEM(record.shape, f32),
                pltpu.VMEM((2, 2, width + 8, across + 2 * PAD, downward), f32),
                pltpu.VMEM((width, survey, downward), f32),
                pltpu.VMEM((width, across, downward), f32),
                pltpu.VMEM((width, across, downward), f32),
                pltpu.VMEM((2, width, across, downward), f32),
                pltpu.VMEM((width, across + 2 * margin, downward), f32),
                pltpu.VMEM((4, 2 * n_shot - 1) + piece[1:], f32),
                pltpu.VMEM((4, 2 * n_shot - 1) + piece[1:], f32),
                pltpu.VMEM((n_shot - 1, n_pair) + piece, f32),
                pltpu.VMEM(velocity.shape, f32),
                pltpu.VMEM((2, width, across, downward), f32),
                dma((4,)),
                dma((4,)),
                dma((2, 2)),
                dma((2, 2, CHUNKS)),
                dma((1,)),
                dma((4,)),
                dma((n_shot - 1, 2)),
                dma((n_shot - 1, 3)),
                dma((n_shot,)),
                dma((n_shot,)),
                dma((1,)),
                dma((4,)),
                dma((n_shot - 1,)),
                dma((n_shot - 1,)),
            ],
            compiler_params=pltpu.CompilerParams(
                collective_id=0, has_side_effects=True, vmem_limit_bytes=40 * 1024 * 1024
            ),
        )(*[
            pltpu.with_memory_space_constraint(operand, pltpu.HBM) if operand.size > 1 else operand
            for operand in (
                anchors, source_x, source_yz, wavelet, recv_x, recv_yz, record,
                velocity, source_prev, source_now, recv_prev, recv_now,
            )
        ])

        return pl.pallas_call(
            deliver,
            out_shape=[jax.ShapeDtypeStruct(shape, f32) for shape in shapes],
            in_specs=[vmem] * 4,
            out_specs=[anywhere] * 3,
            scratch_shapes=[pltpu.VMEM(velocity.shape, f32), dma((3,))],
        )(*[pltpu.with_memory_space_constraint(result, pltpu.VMEM) for result in results])

    in_specs = (
        P(("region", "tile"), ("shot", "pair"), None),
        P(("region", "shot")),
        P(("region", "shot", "pair"), "tile", None, None),
        P(("region", "shot", "pair"), "tile", None, None),
        P(("region", "shot", "pair"), "tile", None, None),
        P(("region", "shot", "pair"), "tile", None, None),
        P(("region", "shot", "pair")),
        P(("region", "shot", "pair")),
        P(("region", "shot", "pair"), None),
        P(("region", "shot", "pair"), None),
        P(("region", "shot", "pair"), None),
        P(("region", "shot", "pair"), None, None),
    )
    out_specs = (
        P(("region", "tile"), ("shot", "pair"), None),
        P(("region", "shot", "pair"), "tile", None, None),
        P(("region", "shot", "pair"), "tile", None, None),
    )
    return jax.shard_map(shards, mesh=mesh, in_specs=in_specs, out_specs=out_specs, check_vma=False)
```
